128 devices in a mesh: row: 8 (over z, core), col: 16 (over y, x).
Axes of the slice: x: 4, y: 4, z: 4, core: 2. Of those that a mesh axis runs over, the one named last changes fastest.
Arguments:
- panel_first: bfloat16 [128, 256, 1024], P(('row', 'col')), may hold values from -3 to 3
- panel_second: bfloat16 [128, 256, 1024], P(('row', 'col')), may hold values from -4 to 4
- diag_first: bfloat16 [1024, 1024], P('col'), as said below
- bridge: bfloat16 [1024, 1024], P('col'), may hold values from -0.024902344 to 0.024902344
- diag_second: bfloat16 [1024, 1024], P('col'), as said below
- trailing: float32 [128, 24, 256, 256], P(('row', 'col')), may hold values from -6 to 6
- trail_pairs: int32 [128, 2, 24], P(('row', 'col')), may hold values from 0 to 15, as said below
- live_count: int32 [128], P(('row', 'col')), may hold values from 1 to 24, as said below
Outputs:
- lower_first: bfloat16 [128, 256, 1024], P(('row', 'col'))
- lower_second: bfloat16 [128, 256, 1024], P(('row', 'col'))
- trailing_out: float32 [128, 24, 256, 256], P(('row', 'col'))
The draws below stay inside these ranges and needn't reach their ends.
Inputs may be any that keep to these rules, and one draw needn't show every extreme that they name: `trail_pairs`: on each device the listed pairs are distinct; the first entry of a pair is below 16 and the second below 8. `live_count`: some device has all 24 slots live in every draw. `diag_first`: symmetric and positive definite, with diagonal entries between 0.75 and 2.3. `diag_second`: symmetric and positive definite, with diagonal entries between 3.4 and 7.5.
All inputs are finite; a program needn't handle non-finite values.
Results may differ from the reference program's by a relative error of at most 0.001.
Values may be sent and summed in bfloat16 or wider, within the bound.
No kernel may reach another device: no remote copies, remote signals or barrier semaphores. Data moves between devices by JAX's collectives and lax.ppermute only.
A program may use at most 192 MiB of HBM per device.

```python
import jax
import jax.numpy as jnp
from jax import lax

PANEL = 1024
TILE = 256
SLOTS = 24
PTILES = 128
N_ROW = 8
N_COL = 16


def definite_block(base_key, low_diag, high_diag, unit_part, low_load, high_load, rough_total):
    rough_key, scale_key, load_key = jax.random.split(base_key, 3)
    group = max(PANEL // 16, 1)
    limit = rough_total / (PANEL - 1)
    raw = jax.random.uniform(rough_key, (PANEL, PANEL), jnp.float32, -limit, limit)
    upper = jnp.triu(raw, 1)
    rough = upper + upper.T
    load = jax.random.uniform(load_key, (PANEL,), jnp.float32, low_load, high_load)
    member = jnp.arange(PANEL) // group
    same = member[:, None] == member[None, :]
    shared = jnp.where(same, load[:, None] * load[None, :], 0.0)
    core = rough + shared + unit_part * jnp.eye(PANEL, dtype=jnp.float32)
    scale = jax.random.uniform(scale_key, (PANEL,), jnp.float32, low_diag, high_diag)
    root = jnp.sqrt(scale)
    outer = root[:, None] * root[None, :]
    return (outer * core).astype(jnp.bfloat16)


def draw_diag_first(key, part):
    return definite_block(jax.random.fold_in(key, 11), 1.0, 2.0, 0.5, 0.5, 0.8, 0.15)


def draw_diag_second(key, part):
    return definite_block(jax.random.fold_in(key, 12), 3.0, 5.0, 1.0, 0.4, 0.7, 0.3)


def draw_bridge(key, part):
    values = jax.random.uniform(jax.random.fold_in(key, 15), (PANEL, PANEL), jnp.float32, -0.026, 0.026)
    values = jnp.clip(values, -0.02490234375, 0.02490234375)
    return values.astype(jnp.bfloat16)


def draw_trail_pairs(key, part):
    key_list = jax.random.split(jax.random.fold_in(key, 13), PTILES)

    def one_list(single_key):
        shuffled = jax.random.permutation(single_key, N_ROW * N_COL)[:SLOTS]
        return jnp.stack([shuffled // N_ROW, shuffled % N_ROW]).astype(jnp.int32)
    return jax.vmap(one_list)(key_list)


def draw_live_count(key, part):
    base_key, heavy_key, pick_key = jax.random.split(jax.random.fold_in(key, 14), 3)
    modest = jax.random.randint(base_key, (PTILES,), 1, SLOTS // 2 + 1)
    heavy = jax.random.randint(heavy_key, (PTILES,), 0, 8) == 0
    chosen = jax.random.randint(pick_key, (), 0, PTILES)
    loaded = heavy | (jnp.arange(PTILES) == chosen)
    return jnp.where(loaded, SLOTS, modest).astype(jnp.int32)


def levels(stream_key, shape, shards, smallest, top_value):
    gain, own = 1.0, jax.random.fold_in(stream_key, 6)
    for axis_at, shards_of in shards:
        draws = jnp.exp(jax.random.uniform(jax.random.fold_in(own, axis_at), (shards_of,), jnp.float32, smallest / len(shards), top_value / len(shards)))
        gain = gain * jnp.repeat(draws, shape[axis_at] // shards_of).reshape([-1 if axis == axis_at else 1 for axis in range(len(shape))])
    return gain


def normal_values(stream_key, shape, width, bound, shards=(), held_as=jnp.bfloat16):
    drawn = width * jax.random.normal(stream_key, shape, jnp.float32)
    if shards:
        drawn = drawn * levels(stream_key, shape, shards, -0.22, 0.18)
    return jnp.clip(drawn, -bound, bound).astype(held_as)


def setup_inputs(seed: int = 0) -> dict:
    key_of = jax.random.split(jax.random.key(seed), 9)
    return {
        "panel_first": normal_values(key_of[0], (PTILES, TILE, PANEL), 0.2, 3.0, ((0, 128),)),
        "panel_second": normal_values(key_of[1], (PTILES, TILE, PANEL), 0.3, 4.0, ((0, 128),)),
        "diag_first": draw_diag_first(jax.random.fold_in(key_of[8], 71), 0),
        "bridge": draw_bridge(jax.random.fold_in(key_of[8], 71), 0),
        "diag_second": draw_diag_second(jax.random.fold_in(key_of[8], 71), 0),
        "trailing": normal_values(key_of[5], (PTILES, SLOTS, TILE, TILE), 1.0, 6.0, ((0, 128),), jnp.float32),
        "trail_pairs": draw_trail_pairs(jax.random.fold_in(key_of[8], 71), 0),
        "live_count": draw_live_count(jax.random.fold_in(key_of[8], 71), 0),
    }


def right_solve(lower_factor, block_rows):
    return jax.scipy.linalg.solve_triangular(lower_factor, block_rows.T, lower=True).T

def reference(panel_first, panel_second, diag_first, bridge, diag_second, trailing, trail_pairs, live_count):
    highest = lax.Precision.HIGHEST
    factor_first = jnp.linalg.cholesky(diag_first.astype(jnp.float32))
    coupling = right_solve(factor_first, bridge.astype(jnp.float32))
    shifted = diag_second.astype(jnp.float32) - jnp.dot(coupling.astype(jnp.float32), coupling.T.astype(jnp.float32), precision=highest, preferred_element_type=jnp.float32)
    factor_second = jnp.linalg.cholesky(shifted)
    flat_first = panel_first.astype(jnp.float32).reshape(PTILES * TILE, PANEL)
    lower_first = right_solve(factor_first, flat_first).astype(jnp.bfloat16)
    flat_second = panel_second.astype(jnp.float32).reshape(PTILES * TILE, PANEL)
    reduced = flat_second - jnp.dot(lower_first.astype(jnp.float32), coupling.T.astype(jnp.float32), precision=highest, preferred_element_type=jnp.float32)
    lower_second = right_solve(factor_second, reduced).astype(jnp.bfloat16)
    lower_first = lower_first.reshape(PTILES, TILE, PANEL)
    lower_second = lower_second.reshape(PTILES, TILE, PANEL)
    stacked = jnp.concatenate([lower_first, lower_second], axis=2).astype(jnp.float32)

    def one_device(packed):
        device_index, tiles_in, pair_list, live_slots = packed
        grid_row = device_index // N_COL
        grid_col = device_index % N_COL
        left_tiles = stacked[(grid_row * N_COL + pair_list[0]).astype(jnp.int32)]
        right_tiles = stacked[(pair_list[1] * N_COL + grid_col).astype(jnp.int32)]
        products = jnp.einsum('sik,sjk->sij', left_tiles, right_tiles, precision=highest)
        active = (jnp.arange(SLOTS, dtype=jnp.int32) < live_slots)[:, None, None]
        return tiles_in - jnp.where(active, products, jnp.zeros_like(products))
    trailing_out = lax.map(one_device, (jnp.arange(PTILES, dtype=jnp.int32), trailing, trail_pairs, live_count))
    return (lower_first, lower_second, trailing_out)
```

```python
import jax
import jax.numpy as jnp
from jax import lax
from jax.experimental import pallas as pl
from jax.experimental.pallas import tpu as pltpu
from jax.sharding import PartitionSpec as P

F32, BF16 = jnp.float32, jnp.bfloat16
N, NB, Q = 1024, 128, 8


def split(x):
    hi = x.astype(BF16)
    return hi, (x - hi.astype(F32)).astype(BF16)


def dot(a, b, dims):
    return lax.dot_general(a, b, (dims, ((), ())), preferred_element_type=F32)


def diag_inverse(tiles):
    count = len(tiles)
    shape = (Q, NB)
    sub = lax.broadcasted_iota(jnp.int32, shape, 0)
    lane = lax.broadcasted_iota(jnp.int32, shape, 1)
    wide = lambda v: jnp.broadcast_to(v, shape)
    tiles = list(tiles)
    out = []
    for s in range(count):
        c0 = Q * s
        blk = tiles[s]
        cols = [wide(blk[:, c0 + m : c0 + m + 1]) for m in range(Q)]
        e = {(i, m): wide(cols[m][i : i + 1, :]) for m in range(Q) for i in range(m, Q)}
        r, l, v = [], {}, {}
        for m in range(Q):
            rm = lax.rsqrt(e[m, m])
            r.append(rm)
            for i in range(m + 1, Q):
                l[i, m] = e[i, m] * rm
            for j in range(m + 1, Q):
                for i in range(j, Q):
                    e[i, j] = e[i, j] - l[i, m] * l[j, m]
        for m in range(Q):
            v[m, m] = r[m]
            for i in range(m + 1, Q):
                acc = l[i, m] * v[m, m]
                for k in range(m + 1, i):
                    acc = acc + l[i, k] * v[k, m]
                v[i, m] = -(r[i] * acc)
        inside = (lane >= c0) & (lane < c0 + Q)
        tb = jnp.where(inside, jnp.where(lane - c0 == sub, 1.0, 0.0), blk)

        def combine(coef, src):
            total = None
            for k in range(Q):
                col = jnp.zeros(shape, F32)
                for i in range(Q):
                    got = coef(i, k)
                    if got is not None:
                        col = jnp.where(sub == i, got, col)
                term = col * wide(src[k : k + 1, :])
                total = term if total is None else total + term
            return total

        w = combine(lambda i, k: v[i, k] if i >= k else None, tb)
        out.append(jnp.where(lane < c0 + Q, w, 0.0))
        if s + 1 < count:
            z = combine(lambda i, k: v[k, i] if i <= k else None, w)
            zr = [wide(z[m : m + 1, :]) for m in range(Q)]
            for t in range(s + 1, count):
                row = tiles[t]
                total = None
                for m in range(Q):
                    term = wide(row[:, c0 + m : c0 + m + 1]) * zr[m]
                    total = term if total is None else total + term
                tiles[t] = jnp.where(inside, 0.0, row) - total
    return out


def factor(load_row, rh, rl, tri, start=None):
    blocks = N // NB
    lane = lax.broadcasted_iota(jnp.int32, (NB, N), 1)
    K0 = ((0,), (0,))
    KM = ((1,), (0,))

    def step(k, carry):
        k0 = pl.multiple_of(k * NB, NB)
        tri[...] = jnp.where(lane >= k0, load_row(k0), 0.0)
        for kk in range(1, blocks):

            @pl.when(k == kk)
            def _():
                h = kk * NB
                ah, al = rh[0:h, h : h + NB], rl[0:h, h : h + NB]
                bh, bl = rh[0:h, :], rl[0:h, :]
                tri[...] -= dot(ah, bh, K0) + dot(ah, bl, K0) + dot(al, bh, K0)
                rh[0:h, h : h + NB] = jnp.zeros((h, NB), BF16)
                rl[0:h, h : h + NB] = jnp.zeros((h, NB), BF16)

        d = tri[:, pl.ds(k0, NB)]
        tiles = diag_inverse([d[Q * i : Q * i + Q, :] for i in range(NB // Q)])
        w = jnp.concatenate(tiles, axis=0)
        tri[:, pl.ds(k0, NB)] = jnp.eye(NB, dtype=F32)
        wh, wl = split(w)
        xh, xl = split(tri[...])
        row = dot(wh, xh, KM) + dot(wh, xl, KM) + dot(wl, xh, KM)
        oh, ol = split(row)
        rh[pl.ds(k0, NB), :] = oh
        rl[pl.ds(k0, NB), :] = ol
        return carry

    lax.fori_loop(0, blocks, step, 0)


def first_kernel(g_ref, oh, ol, tri):
    def load(k0):
        i = k0 // 64
        return jnp.concatenate(
            [g_ref[i, 0:64, :], g_ref[i + 1, 0:64, :]], axis=0
        ).astype(F32)

    factor(load, oh, ol, tri)


def second_kernel(g_ref, w1h, w1l, oh, ol, gh, gl, ch, cl, shifted, tri):
    KT = ((1,), (1,))
    KM = ((1,), (0,))
    half = 256
    for i in range(N // half):
        for j in range(N // half):
            s, t, kk = slice(i * half, i * half + half), slice(j * half, j * half + half), half * (j + 1)
            b = jnp.concatenate([g_ref[4 * i + q, 64:128, 0:kk] for q in range(4)], axis=0)
            hi, lo = split(dot(b, w1h[t, 0:kk], KT) + dot(b, w1l[t, 0:kk], KT))
            ch[s, t] = hi
            cl[s, t] = lo
    for i in range(N // half):
        for j in range(i, N // half):
            s, t = slice(i * half, i * half + half), slice(j * half, j * half + half)
            d = jnp.concatenate([g_ref[4 * i + q, 128:192, t] for q in range(4)], axis=0)
            prod = dot(ch[s, :], ch[t, :], KT) + dot(ch[s, :], cl[t, :], KT) + dot(cl[s, :], ch[t, :], KT)
            shifted[s, t] = d.astype(F32) - prod
    factor(lambda k0: shifted[pl.ds(k0, NB), :], oh, ol, tri)
    for i in range(N // half):
        for j in range(N // half):
            s, t, kk = slice(i * half, i * half + half), slice(j * half, j * half + half), half * (i + 1)
            hi, lo = split(
                dot(oh[s, 0:kk], ch[0:kk, t], KM)
                + dot(oh[s, 0:kk], cl[0:kk, t], KM)
                + dot(ol[s, 0:kk], ch[0:kk, t], KM)
            )
            gh[s, t] = hi
            gl[s, t] = lo


VM = pl.BlockSpec(memory_space=pltpu.VMEM)
LIMIT = 60 * 1024 * 1024


def first_stage(g):
    return pl.pallas_call(
        first_kernel,
        out_shape=[jax.ShapeDtypeStruct((N, N), BF16)] * 2,
        in_specs=[VM],
        out_specs=[VM] * 2,
        scratch_shapes=[pltpu.VMEM((NB, N), F32)],
        compiler_params=pltpu.CompilerParams(vmem_limit_bytes=LIMIT),
        cost_estimate=pl.CostEstimate(flops=10**10, bytes_accessed=10**7, transcendentals=0),
        name="first_stage",
    )(g)


def second_stage(g, w1h, w1l):
    return pl.pallas_call(
        second_kernel,
        out_shape=[jax.ShapeDtypeStruct((N, N), BF16)] * 4,
        in_specs=[VM] * 3,
        out_specs=[VM] * 4,
        scratch_shapes=[pltpu.VMEM((N, N), BF16)] * 2
        + [pltpu.VMEM((N, N), F32)]
        + [pltpu.VMEM((NB, N), F32)],
        compiler_params=pltpu.CompilerParams(vmem_limit_bytes=LIMIT),
        cost_estimate=pl.CostEstimate(flops=2 * 10**10, bytes_accessed=10**7, transcendentals=0),
        name="second_stage",
    )(g, w1h, w1l)


PER, GROUP = 2, 4


def final_kernel(
    pairs, live, need_col, need_row, own,
    col_p, row_p, w1h, w1l, w2h, w2l, gh, gl, tin,
    own_first, own_second, tout, lcol, lrow,
):
    KT = ((1,), (1,))
    step = pl.program_id(0)
    half = 256
    ncol, nrow = lcol.shape[0] // PER, lrow.shape[0] // PER

    def solve(src, dst, base):
        p1 = jnp.concatenate([src[u, 0] for u in range(PER)], axis=0)
        for j in range(N // half):
            t, kk = slice(j * half, j * half + half), half * (j + 1)
            got = dot(p1[:, 0:kk], w1h[t, 0:kk], KT) + dot(p1[:, 0:kk], w1l[t, 0:kk], KT)
            got = got.astype(BF16)
            for u in range(PER):
                dst[base + u, :, t] = got[u * half : u * half + half, :]
        p2 = jnp.concatenate([src[u, 1] for u in range(PER)], axis=0)
        l1 = jnp.concatenate([dst[base + u, :, 0:N] for u in range(PER)], axis=0)
        for j in range(N // half):
            t, kk = slice(j * half, j * half + half), half * (j + 1)
            got = dot(p2[:, 0:kk], w2h[t, 0:kk], KT) + dot(p2[:, 0:kk], w2l[t, 0:kk], KT)
            got = got - (dot(l1, gh[t, :], KT) + dot(l1, gl[t, :], KT))
            got = got.astype(BF16)
            for u in range(PER):
                dst[base + u, :, N + j * half : N + j * half + half] = got[u * half : u * half + half, :]

    @pl.when(step < ncol)
    def _():
        @pl.when(need_col[jnp.minimum(step, ncol - 1)] > 0)
        def _():
            solve(col_p, lcol, PER * step)

    @pl.when((step >= ncol) & (step < ncol + nrow))
    def _():
        at = jnp.clip(step - ncol, 0, nrow - 1)

        @pl.when(need_row[at] > 0)
        def _():
            solve(row_p, lrow, PER * at)

    @pl.when(step == ncol + nrow - 1)
    def _():
        own_first[0] = lrow[own[0], :, 0:N]
        own_second[0] = lrow[own[0], :, N : 2 * N]

    @pl.when(step >= ncol + nrow)
    def _():
        base = (step - ncol - nrow) * GROUP
        for u in range(GROUP):
            slot = base + u

            @pl.when(slot < live[0])
            def _():
                a, b = pairs[slot], pairs[24 + slot]
                tout[0, u] = tin[0, u] - dot(lrow[a], lcol[b], KT)

            @pl.when(slot >= live[0])
            def _():
                tout[0, u] = tin[0, u]


def final_stage(pairs, live, need_col, need_row, own, col_p, row_p, weights, trailing):
    ncol, nrow = col_p.shape[0], row_p.shape[0]
    slots = trailing.shape[1]
    cs, rs = ncol // PER, nrow // PER
    ks = slots // GROUP
    tiles = lambda lo, cnt: (lambda s, *_: (jnp.clip(s - lo, 0, cnt - 1), 0, 0, 0))
    tmap = lambda s, *_: (0, jnp.clip(s - cs - rs, 0, ks - 1), 0, 0)
    once = pl.BlockSpec((N, N), lambda s, *_: (0, 0), pipeline_mode=pl.Buffered(1))
    own_spec = pl.BlockSpec((1, 256, N), lambda s, *_: (0, 0, 0))
    return pl.pallas_call(
        final_kernel,
        out_shape=[
            jax.ShapeDtypeStruct((1, 256, N), BF16),
            jax.ShapeDtypeStruct((1, 256, N), BF16),
            jax.ShapeDtypeStruct(trailing.shape, F32),
        ],
        grid_spec=pltpu.PrefetchScalarGridSpec(
            num_scalar_prefetch=5,
            grid=(cs + rs + ks,),
            in_specs=[
                pl.BlockSpec((PER, 2, 256, N), tiles(0, cs)),
                pl.BlockSpec((PER, 2, 256, N), tiles(cs, rs)),
            ]
            + [once] * 6
            + [pl.BlockSpec((1, GROUP, 256, 256), tmap)],
            out_specs=[own_spec, own_spec, pl.BlockSpec((1, GROUP, 256, 256), tmap)],
            scratch_shapes=[pltpu.VMEM((ncol, 256, 2 * N), BF16), pltpu.VMEM((nrow, 256, 2 * N), BF16)],
        ),
        compiler_params=pltpu.CompilerParams(
            vmem_limit_bytes=LIMIT, dimension_semantics=("arbitrary",)
        ),
        cost_estimate=pl.CostEstimate(flops=6 * 10**10, bytes_accessed=4 * 10**7, transcendentals=0),
        name="final_stage",
    )(pairs, live, need_col, need_row, own, col_p, row_p, *weights, trailing)


def per_device(
    panel_first, panel_second, diag_first, bridge, diag_second, trailing, trail_pairs, live_count
):
    blocks = lax.all_gather(
        jnp.concatenate([diag_first, bridge, diag_second], axis=0), "col", axis=0
    )
    both = jnp.stack([panel_first[0], panel_second[0]], axis=0)
    row_p = lax.all_gather(both, "col", axis=0)
    col_p = lax.all_gather(both, "row", axis=0)
    own = lax.axis_index("col").astype(jnp.int32)
    pairs = trail_pairs[0]
    active = jnp.arange(pairs.shape[1], dtype=jnp.int32) < live_count[0]
    group_r = jnp.arange(row_p.shape[0] // PER, dtype=jnp.int32)
    group_c = jnp.arange(col_p.shape[0] // PER, dtype=jnp.int32)
    need_row = jnp.any((pairs[0][None] // PER == group_r[:, None]) & active[None], axis=1) | (group_r == own // PER)
    need_col = jnp.any((pairs[1][None] // PER == group_c[:, None]) & active[None], axis=1)
    w1h, w1l = first_stage(blocks)
    w2h, w2l, gh, gl = second_stage(blocks, w1h, w1l)
    return final_stage(
        pairs.reshape(-1), live_count, need_col.astype(jnp.int32), need_row.astype(jnp.int32), own[None],
        col_p, row_p, (w1h, w1l, w2h, w2l, gh, gl), trailing,
    )


def solution(mesh):
    return jax.shard_map(
        per_device,
        mesh=mesh,
        in_specs=(
            P(("row", "col"), None, None),
            P(("row", "col"), None, None),
            P("col", None),
            P("col", None),
            P("col", None),
            P(("row", "col"), None, None, None),
            P(("row", "col"), None, None),
            P(("row", "col")),
        ),
        out_specs=(
            P(("row", "col"), None, None),
            P(("row", "col"), None, None),
            P(("row", "col"), None, None, None),
        ),
        check_vma=False,
    )
```

```python
import functools

import jax
import jax.numpy as jnp
from jax import lax
from jax.experimental import pallas as pl
from jax.experimental.pallas import tpu as pltpu
from jax.sharding import PartitionSpec as P

F32, BF16 = jnp.float32, jnp.bfloat16
N, NB, Q = 1024, 128, 8


def split(x):
    hi = x.astype(BF16)
    return hi, (x - hi.astype(F32)).astype(BF16)


def dot(a, b, dims):
    return lax.dot_general(a, b, (dims, ((), ())), preferred_element_type=F32)


def diag_inverse(tiles):
    count = len(tiles)
    shape = (Q, NB)
    sub = lax.broadcasted_iota(jnp.int32, shape, 0)
    lane = lax.broadcasted_iota(jnp.int32, shape, 1)
    wide = lambda v: jnp.broadcast_to(v, shape)
    lanes = lambda v, c: jnp.take_along_axis(v, jnp.full(shape, c, jnp.int32), axis=1)
    tiles = list(tiles)
    out = []
    for s in range(count):
        c0 = Q * s
        blk = tiles[s]
        cols = [lanes(blk, c0 + m) for m in range(Q)]
        e = {(i, m): wide(cols[m][i : i + 1, :]) for m in range(Q) for i in range(m, Q)}
        r, l, v = [], {}, {}
        for m in range(Q):
            rm = lax.rsqrt(e[m, m])
            r.append(rm)
            for i in range(m + 1, Q):
                l[i, m] = e[i, m] * rm
            for j in range(m + 1, Q):
                for i in range(j, Q):
                    e[i, j] = e[i, j] - l[i, m] * l[j, m]
        for m in range(Q):
            v[m, m] = r[m]
            for i in range(m + 1, Q):
                acc = l[i, m] * v[m, m]
                for k in range(m + 1, i):
                    acc = acc + l[i, k] * v[k, m]
                v[i, m] = -(r[i] * acc)
        inside = (lane >= c0) & (lane < c0 + Q)
        tb = jnp.where(inside, jnp.where(lane - c0 == sub, 1.0, 0.0), blk)

        def combine(coef, src):
            total = None
            for k in range(Q):
                col = jnp.zeros(shape, F32)
                for i in range(Q):
                    got = coef(i, k)
                    if got is not None:
                        col = jnp.where(sub == i, got, col)
                term = col * wide(src[k : k + 1, :])
                total = term if total is None else total + term
            return total

        w = combine(lambda i, k: v[i, k] if i >= k else None, tb)
        out.append(jnp.where(lane < c0 + Q, w, 0.0))
        if s + 1 < count:
            z = combine(lambda i, k: v[k, i] if i <= k else None, w)
            zr = [wide(z[m : m + 1, :]) for m in range(Q)]
            for t in range(s + 1, count):
                row = tiles[t]
                total = None
                for m in range(Q):
                    term = lanes(row, c0 + m) * zr[m]
                    total = term if total is None else total + term
                tiles[t] = jnp.where(inside, 0.0, row) - total
    return out


def factor(load_row, rh, rl, tri, start=None):
    blocks = N // NB
    lane = lax.broadcasted_iota(jnp.int32, (NB, N), 1)
    K0 = ((0,), (0,))
    KM = ((1,), (0,))

    def step(k, carry):
        k0 = pl.multiple_of(k * NB, NB)
        tri[...] = jnp.where(lane >= k0, load_row(k0), 0.0)
        for kk in range(1, blocks):

            @pl.when(k == kk)
            def _():
                h = kk * NB
                ah, al = rh[0:h, h : h + NB], rl[0:h, h : h + NB]
                bh, bl = rh[0:h, :], rl[0:h, :]
                tri[...] -= dot(ah, bh, K0) + dot(ah, bl, K0) + dot(al, bh, K0)
                rh[0:h, h : h + NB] = jnp.zeros((h, NB), BF16)
                rl[0:h, h : h + NB] = jnp.zeros((h, NB), BF16)

        d = tri[:, pl.ds(k0, NB)]
        tiles = diag_inverse([d[Q * i : Q * i + Q, :] for i in range(NB // Q)])
        w = jnp.concatenate(tiles, axis=0)
        tri[:, pl.ds(k0, NB)] = jnp.eye(NB, dtype=F32)
        wh, wl = split(w)
        xh, xl = split(tri[...])
        row = dot(wh, xh, KM) + dot(wh, xl, KM) + dot(wl, xh, KM)
        oh, ol = split(row)
        rh[pl.ds(k0, NB), :] = oh
        rl[pl.ds(k0, NB), :] = ol
        return carry

    lax.fori_loop(0, blocks, step, 0)


def first_kernel(g_ref, oh, ol, tri):
    def load(k0):
        return g_ref[pl.ds(k0, NB), :].astype(F32)

    factor(load, oh, ol, tri)


def second_kernel(where, mine, theirs, w1h, w1l, oh, ol, gh, gl, ch, cl, shifted, tri, bridge, diag):
    KT = ((1,), (1,))
    KM = ((1,), (0,))
    half = 256
    shard = N // where.shape[0]
    for i in range(where.shape[0]):
        at = where[i]
        rows = slice(i * shard, i * shard + shard)
        for base, ref in ((0, mine), (mine.shape[0], theirs)):

            @pl.when((at >= base) & (at < base + ref.shape[0]))
            def _():
                got = ref[jnp.clip(at - base, 0, ref.shape[0] - 1)]
                bridge[rows, :] = got[0:shard]
                diag[rows, :] = got[shard : 2 * shard]

    for i in range(N // half):
        for j in range(N // half):
            s, t, kk = slice(i * half, i * half + half), slice(j * half, j * half + half), half * (j + 1)
            b = bridge[s, 0:kk]
            hi, lo = split(dot(b, w1h[t, 0:kk], KT) + dot(b, w1l[t, 0:kk], KT))
            ch[s, t] = hi
            cl[s, t] = lo
    for i in range(N // half):
        for j in range(i, N // half):
            s, t = slice(i * half, i * half + half), slice(j * half, j * half + half)
            d = diag[s, t]
            prod = dot(ch[s, :], ch[t, :], KT) + dot(ch[s, :], cl[t, :], KT) + dot(cl[s, :], ch[t, :], KT)
            shifted[s, t] = d.astype(F32) - prod
    factor(lambda k0: shifted[pl.ds(k0, NB), :], oh, ol, tri)
    for i in range(N // half):
        for j in range(N // half):
            s, t, kk = slice(i * half, i * half + half), slice(j * half, j * half + half), half * (i + 1)
            hi, lo = split(
                dot(oh[s, 0:kk], ch[0:kk, t], KM)
                + dot(oh[s, 0:kk], cl[0:kk, t], KM)
                + dot(ol[s, 0:kk], ch[0:kk, t], KM)
            )
            gh[s, t] = hi
            gl[s, t] = lo


VM = pl.BlockSpec(memory_space=pltpu.VMEM)
LIMIT = 60 * 1024 * 1024


def first_stage(g):
    return pl.pallas_call(
        first_kernel,
        out_shape=[jax.ShapeDtypeStruct((N, N), BF16)] * 2,
        in_specs=[VM],
        out_specs=[VM] * 2,
        scratch_shapes=[pltpu.VMEM((NB, N), F32)],
        compiler_params=pltpu.CompilerParams(vmem_limit_bytes=LIMIT),
        cost_estimate=pl.CostEstimate(flops=10**10, bytes_accessed=10**7, transcendentals=0),
        name="first_stage",
    )(g)


def second_stage(where, mine, theirs, w1h, w1l):
    return pl.pallas_call(
        second_kernel,
        out_shape=[jax.ShapeDtypeStruct((N, N), BF16)] * 4,
        in_specs=[pl.BlockSpec(memory_space=pltpu.SMEM)] + [VM] * 4,
        out_specs=[VM] * 4,
        scratch_shapes=[pltpu.VMEM((N, N), BF16)] * 2
        + [pltpu.VMEM((N, N), F32)]
        + [pltpu.VMEM((NB, N), F32)]
        + [pltpu.VMEM((N, N), BF16)] * 2,
        compiler_params=pltpu.CompilerParams(vmem_limit_bytes=LIMIT),
        cost_estimate=pl.CostEstimate(flops=2 * 10**10, bytes_accessed=10**7, transcendentals=0),
        name="second_stage",
    )(where, mine, theirs, w1h, w1l)


PER, GROUP = 2, 4
HALF = 256


def solve_tiles(src, w1h, w1l, w2h, w2l, gh, gl, put):
    KT = ((1,), (1,))
    p1 = jnp.concatenate([src[u, 0] for u in range(PER)], axis=0)
    p2 = jnp.concatenate([src[u, 1] for u in range(PER)], axis=0)
    parts = []
    for j in range(N // HALF):
        t, kk = slice(j * HALF, j * HALF + HALF), HALF * (j + 1)
        got = dot(p1[:, 0:kk], w1h[t, 0:kk], KT) + dot(p1[:, 0:kk], w1l[t, 0:kk], KT)
        parts.append(got.astype(BF16))
        put(j * HALF, parts[-1])
    l1 = jnp.concatenate(parts, axis=1)
    for j in range(N // HALF):
        t, kk = slice(j * HALF, j * HALF + HALF), HALF * (j + 1)
        got = dot(p2[:, 0:kk], w2h[t, 0:kk], KT) + dot(p2[:, 0:kk], w2l[t, 0:kk], KT)
        got = got - (dot(l1, gh[t, :], KT) + dot(l1, gl[t, :], KT))
        put(N + j * HALF, got.astype(BF16))


def rows_kernel(need, own, src, w1h, w1l, w2h, w2l, gh, gl, own_first, own_second, out):
    step = pl.program_id(0)

    @pl.when(need[step] > 0)
    def _():
        def put(c, val):
            for u in range(PER):
                out[u, :, c : c + HALF] = val[u * HALF : u * HALF + HALF, :]

        solve_tiles(src, w1h, w1l, w2h, w2l, gh, gl, put)

    for u in range(PER):

        @pl.when(own[0] == step * PER + u)
        def _():
            own_first[0] = out[u, :, 0:N]
            own_second[0] = out[u, :, N : 2 * N]


ONCE = pl.BlockSpec((N, N), lambda s, *_: (0, 0), pipeline_mode=pl.Buffered(1))


def rows_stage(need, own, src, weights):
    count = src.shape[0]
    own_spec = pl.BlockSpec((1, HALF, N), lambda s, *_: (0, 0, 0))
    return pl.pallas_call(
        rows_kernel,
        out_shape=[
            jax.ShapeDtypeStruct((1, HALF, N), BF16),
            jax.ShapeDtypeStruct((1, HALF, N), BF16),
            jax.ShapeDtypeStruct((count, HALF, 2 * N), BF16),
        ],
        grid_spec=pltpu.PrefetchScalarGridSpec(
            num_scalar_prefetch=2,
            grid=(count // PER,),
            in_specs=[pl.BlockSpec((PER, 2, HALF, N), lambda s, *_: (s, 0, 0, 0))] + [ONCE] * 6,
            out_specs=[own_spec, own_spec, pl.BlockSpec((PER, HALF, 2 * N), lambda s, *_: (s, 0, 0))],
        ),
        compiler_params=pltpu.CompilerParams(vmem_limit_bytes=LIMIT, dimension_semantics=("arbitrary",)),
        cost_estimate=pl.CostEstimate(flops=4 * 10**10, bytes_accessed=4 * 10**7, transcendentals=0),
        name="rows_stage",
    )(need, own, src, *weights)


def final_kernel(pairs, live, need, src, w1h, w1l, w2h, w2l, gh, gl, rows, tin, tout, lcol, lrow, sem):
    KT = ((1,), (1,))
    step = pl.program_id(0)
    ncol = lcol.shape[0] // PER
    fetch = pltpu.make_async_copy(rows, lrow, sem)

    @pl.when(step == 0)
    def _():
        fetch.start()

    @pl.when(step < ncol)
    def _():
        at = jnp.minimum(step, ncol - 1)

        @pl.when(need[at] > 0)
        def _():
            def put(c, val):
                for u in range(PER):
                    lcol[at * PER + u, :, c : c + HALF] = val[u * HALF : u * HALF + HALF, :]

            solve_tiles(src, w1h, w1l, w2h, w2l, gh, gl, put)

    @pl.when(step == ncol)
    def _():
        fetch.wait()

    @pl.when(step >= ncol)
    def _():
        base = (step - ncol) * GROUP
        for u in range(GROUP):
            slot = base + u

            @pl.when(slot < live[0])
            def _():
                a, b = pairs[slot], pairs[24 + slot]
                tout[0, u] = tin[0, u] - dot(lrow[a], lcol[b], KT)

            @pl.when(slot >= live[0])
            def _():
                tout[0, u] = tin[0, u]


def final_stage(pairs, live, need, src, weights, rows, trailing):
    count, slots = src.shape[0], trailing.shape[1]
    cs, ks = count // PER, slots // GROUP
    tmap = lambda s, *_: (0, jnp.clip(s - cs, 0, ks - 1), 0, 0)
    return pl.pallas_call(
        final_kernel,
        out_shape=jax.ShapeDtypeStruct(trailing.shape, F32),
        grid_spec=pltpu.PrefetchScalarGridSpec(
            num_scalar_prefetch=3,
            grid=(cs + ks,),
            in_specs=[pl.BlockSpec((PER, 2, HALF, N), lambda s, *_: (jnp.minimum(s, cs - 1), 0, 0, 0))]
            + [ONCE] * 6
            + [pl.BlockSpec(memory_space=pl.ANY), pl.BlockSpec((1, GROUP, HALF, HALF), tmap)],
            out_specs=pl.BlockSpec((1, GROUP, HALF, HALF), tmap),
            scratch_shapes=[
                pltpu.VMEM((count, HALF, 2 * N), BF16),
                pltpu.VMEM(rows.shape, BF16),
                pltpu.SemaphoreType.DMA,
            ],
        ),
        compiler_params=pltpu.CompilerParams(vmem_limit_bytes=LIMIT, dimension_semantics=("arbitrary",)),
        cost_estimate=pl.CostEstimate(flops=3 * 10**10, bytes_accessed=4 * 10**7, transcendentals=0),
        name="final_stage",
    )(pairs, live, need, src, *weights, rows, trailing)


def spread(x, nrow, ncol):
    every = [(r, c) for r in range(nrow) for c in range(ncol)]
    half = ncol // 2
    flat = lambda r, c: r % nrow * ncol + c % ncol
    near, away = (
        lax.ppermute(x, ("row", "col"), [(flat(r, c + r + off), flat(r, c)) for r, c in every])
        for off in (0, half)
    )
    unit = jnp.stack([near, away], axis=0)
    up = lax.ppermute(unit, "row", [(r, (r + 2) % nrow) for r in range(nrow)])
    down = lax.ppermute(unit, "row", [(r, (r - 2) % nrow) for r in range(nrow)])
    row, col = lax.axis_index("row"), lax.axis_index("col")
    core = row % 2
    far = lax.ppermute(
        jnp.where(core == 0, up, down), "row", [(r, (r + (2 if r % 2 == 0 else -2)) % nrow) for r in range(nrow)]
    )
    mine = jnp.concatenate([unit, down, far, up], axis=0)
    theirs = lax.ppermute(mine, "row", [(r, r ^ 1) for r in range(nrow)])
    off = (jnp.arange(ncol, dtype=jnp.int32) - col) % ncol
    holder, side = off % half, off // half
    ahead = (holder // 2 - row // 2) % (nrow // 2)
    other = (holder % 2 != core).astype(jnp.int32)
    return mine, theirs, (other * mine.shape[0] + 2 * ahead + side).astype(jnp.int32)


def per_device(
    nrow, ncol, panel_first, panel_second, diag_first, bridge, diag_second, trailing, trail_pairs, live_count
):
    whole_first = lax.all_gather(diag_first, "col", axis=0, tiled=True)
    mine, theirs, where = spread(jnp.concatenate([bridge, diag_second], axis=0), nrow, ncol)
    both = jnp.stack([panel_first[0], panel_second[0]], axis=0)
    row_p = lax.all_gather(both, "col", axis=0)
    col_p = lax.all_gather(both, "row", axis=0)
    own = lax.axis_index("col").astype(jnp.int32)
    pairs = trail_pairs[0]
    active = jnp.arange(pairs.shape[1], dtype=jnp.int32) < live_count[0]
    group_r = jnp.arange(ncol // PER, dtype=jnp.int32)
    group_c = jnp.arange(nrow // PER, dtype=jnp.int32)
    need_row = jnp.any((pairs[0][None] // PER == group_r[:, None]) & active[None], axis=1) | (group_r == own // PER)
    need_col = jnp.any((pairs[1][None] // PER == group_c[:, None]) & active[None], axis=1)
    w1h, w1l = first_stage(whole_first)
    weights = (w1h, w1l, *second_stage(where, mine, theirs, w1h, w1l))
    lower_first, lower_second, rows = rows_stage(need_row.astype(jnp.int32), own[None], row_p, weights)
    owned = final_stage(pairs.reshape(-1), live_count, need_col.astype(jnp.int32), col_p, weights, rows, trailing)
    return lower_first, lower_second, owned


def solution(mesh):
    return jax.shard_map(
        functools.partial(per_device, mesh.shape["row"], mesh.shape["col"]),
        mesh=mesh,
        in_specs=(
            P(("row", "col"), None, None),
            P(("row", "col"), None, None),
            P("col", None),
            P("col", None),
            P("col", None),
            P(("row", "col"), None, None, None),
            P(("row", "col"), None, None),
            P(("row", "col")),
        ),
        out_specs=(
            P(("row", "col"), None, None),
            P(("row", "col"), None, None),
            P(("row", "col"), None, None, None),
        ),
        check_vma=False,
    )
```

```python
import functools

import jax
import jax.numpy as jnp
from jax import lax
from jax.experimental import pallas as pl
from jax.experimental.pallas import tpu as pltpu
from jax.sharding import PartitionSpec as P

F32, BF16 = jnp.float32, jnp.bfloat16
N, NB, Q = 1024, 128, 8


def split(x):
    hi = x.astype(BF16)
    return hi, (x - hi.astype(F32)).astype(BF16)


def dot(a, b, dims):
    return lax.dot_general(a, b, (dims, ((), ())), preferred_element_type=F32)


def diag_inverse(tiles, far_from=None):
    count = len(tiles)
    shape = (Q, NB)
    sub = lax.broadcasted_iota(jnp.int32, shape, 0)
    lane = lax.broadcasted_iota(jnp.int32, shape, 1)
    wide = lambda v: jnp.broadcast_to(v, shape)
    lanes = lambda v, c: jnp.take_along_axis(v, jnp.full(shape, c, jnp.int32), axis=1)
    zero = jnp.zeros(shape, F32)
    tiles = list(tiles)
    out = []

    def total(terms):
        while len(terms) > 1:
            terms = [a + b for a, b in zip(terms[::2], terms[1::2])] + ([terms[-1]] if len(terms) % 2 else [])
        return terms[0]

    def small(e):
        r, l, v = [], {}, {}
        for m in range(Q):
            rm = lax.rsqrt(e[m, m])
            r.append(rm)
            for i in range(m + 1, Q):
                l[i, m] = e[i, m] * rm
            for j in range(m + 1, Q):
                for i in range(j, Q):
                    e[i, j] = e[i, j] - l[i, m] * l[j, m]
            v[m, m] = rm
            for k in range(m):
                v[m, k] = -(rm * total([l[m, j] * v[j, k] for j in range(k, m)]))
        return v

    def assemble(coef):
        cols = []
        for k in range(Q):
            col = zero
            for i in range(Q):
                got = coef(i, k)
                if got is not None:
                    col = jnp.where(sub == i, got, col)
            cols.append(col)
        return cols

    def spread_rows(x):
        return [wide(x[k : k + 1, :]) for k in range(Q)]

    def apply(cols, rows):
        return total([c * x for c, x in zip(cols, rows)])

    for s in range(0, count, 2):
        c0, c1 = Q * s, Q * s + Q
        b0, b1 = tiles[s], tiles[s + 1]
        in0 = (lane >= c0) & (lane < c1)
        in1 = (lane >= c1) & (lane < c1 + Q)
        d0 = [lanes(b0, c0 + m) for m in range(Q)]
        a = [lanes(b1, c0 + m) for m in range(Q)]
        d1 = [lanes(b1, c1 + m) for m in range(Q)]
        v0 = small({(i, m): wide(d0[m][i : i + 1, :]) for m in range(Q) for i in range(m, Q)})
        q, qs = [], []
        for k in range(Q):
            qk = total([a[j] * v0[k, j] for j in range(k + 1)])
            q.append(qk)
            qs.append(spread_rows(qk))
        for m in range(Q):
            d1[m] = d1[m] - total([q[k] * qs[k][m] for k in range(Q)])
        v1 = small({(i, m): wide(d1[m][i : i + 1, :]) for m in range(Q) for i in range(m, Q)})
        t0 = jnp.where(in0, jnp.where(lane - c0 == sub, 1.0, 0.0), jnp.where(in1, 0.0, b0))
        v0t = assemble(lambda i, k: v0[k, i] if i <= k else None)
        w0 = apply(assemble(lambda i, k: v0[i, k] if i >= k else None), spread_rows(t0))
        w0r = spread_rows(w0)
        out.append(jnp.where(lane < c1, w0, 0.0))
        t1 = jnp.where(in0, 0.0, b1) - total([q[k] * w0r[k] for k in range(Q)])
        t1 = jnp.where(in1, jnp.where(lane - c1 == sub, 1.0, 0.0), t1)
        w1 = apply(assemble(lambda i, k: v1[i, k] if i >= k else None), spread_rows(t1))
        out.append(jnp.where(lane < c1 + Q, w1, 0.0))
        if s + 2 < count:
            w1r = spread_rows(w1)
            z1 = apply(assemble(lambda i, k: v1[k, i] if i <= k else None), w1r)
            z1r = spread_rows(z1)
            y = w0 - apply(assemble(lambda i, k: qs[i][k]), z1r)
            zr = spread_rows(apply(v0t, spread_rows(y))) + z1r
            both = in0 | in1
            for t in range(s + 2, count):
                row = tiles[t]
                terms = [lanes(row, c0 + m) * zr[m] for m in range(2 * Q)]
                tiles[t] = jnp.where(both, 0.0, row) - total(terms)
    return out


def factor(load_row, rh, rl, tri, start=None):
    blocks = N // NB
    lane = lax.broadcasted_iota(jnp.int32, (NB, N), 1)
    K0 = ((0,), (0,))
    KM = ((1,), (0,))

    rh[...] = jnp.zeros((N, N), BF16)
    rl[...] = jnp.zeros((N, N), BF16)

    def step(k, carry):
        k0 = pl.multiple_of(k * NB, NB)
        tri[...] = jnp.where(lane >= k0, load_row(k0), 0.0)
        cols = pl.ds(k0, NB)

        def update(p, c):
            rows = pl.ds(pl.multiple_of(p * 2 * NB, 2 * NB), 2 * NB)
            ah, al = rh[rows, cols], rl[rows, cols]
            bh, bl = rh[rows, :], rl[rows, :]
            tri[...] -= dot(ah, bh, K0) + dot(ah, bl, K0) + dot(al, bh, K0)
            return c

        lax.fori_loop(0, (k + 1) // 2, update, 0)
        rh[:, cols] = jnp.zeros((N, NB), BF16)
        rl[:, cols] = jnp.zeros((N, NB), BF16)
        d = tri[:, pl.ds(k0, NB)]
        tiles = diag_inverse([d[Q * i : Q * i + Q, :] for i in range(NB // Q)])
        w = jnp.concatenate(tiles, axis=0)
        tri[:, pl.ds(k0, NB)] = jnp.eye(NB, dtype=F32)
        wh, wl = split(w)
        xh, xl = split(tri[...])
        row = dot(wh, xh, KM) + dot(wh, xl, KM) + dot(wl, xh, KM)
        oh, ol = split(row)
        rh[pl.ds(k0, NB), :] = oh
        rl[pl.ds(k0, NB), :] = ol
        return carry

    lax.fori_loop(0, blocks, step, 0)


def first_kernel(g_ref, oh, ol, tri):
    def load(k0):
        return g_ref[pl.ds(k0, NB), :].astype(F32)

    factor(load, oh, ol, tri)


def second_kernel(where, mine, theirs, w1h, w1l, oh, ol, gh, gl, ch, cl, shifted, tri, bridge, diag):
    KT = ((1,), (1,))
    KM = ((1,), (0,))
    half = 256
    shard = N // where.shape[0]
    for i in range(where.shape[0]):
        at = where[i]
        rows = slice(i * shard, i * shard + shard)
        for base, ref in ((0, mine), (mine.shape[0], theirs)):

            @pl.when((at >= base) & (at < base + ref.shape[0]))
            def _():
                got = ref[jnp.clip(at - base, 0, ref.shape[0] - 1)]
                bridge[rows, :] = got[0:shard]
                diag[rows, :] = got[shard : 2 * shard]

    def couple(i, c):
        rows = pl.ds(pl.multiple_of(i * 2 * half, 2 * half), 2 * half)
        for j in range(N // half):
            t, kk = slice(j * half, j * half + half), half * (j + 1)
            b = bridge[rows, 0:kk]
            hi, lo = split(dot(b, w1h[t, 0:kk], KT) + dot(b, w1l[t, 0:kk], KT))
            ch[rows, t] = hi
            cl[rows, t] = lo
        return c

    lax.fori_loop(0, N // (2 * half), couple, 0)

    def shift(i, c):
        s = pl.ds(pl.multiple_of(i * half, half), half)

        def inner(j, c):
            t = pl.ds(pl.multiple_of(j * half, half), half)
            prod = dot(ch[s, :], ch[t, :], KT) + dot(ch[s, :], cl[t, :], KT) + dot(cl[s, :], ch[t, :], KT)
            shifted[s, t] = diag[s, t].astype(F32) - prod
            return c

        return lax.fori_loop(i, N // half, inner, c)

    lax.fori_loop(0, N // half, shift, 0)
    factor(lambda k0: shifted[pl.ds(k0, NB), :], oh, ol, tri)

    def carry_over(j, c):
        t = pl.ds(pl.multiple_of(j * 2 * half, 2 * half), 2 * half)
        for i in range(N // half):
            s, kk = slice(i * half, i * half + half), half * (i + 1)
            hi, lo = split(
                -(
                    dot(oh[s, 0:kk], ch[0:kk, t], KM)
                    + dot(oh[s, 0:kk], cl[0:kk, t], KM)
                    + dot(ol[s, 0:kk], ch[0:kk, t], KM)
                )
            )
            gh[s, t] = hi
            gl[s, t] = lo
        return c

    lax.fori_loop(0, N // (2 * half), carry_over, 0)


VM = pl.BlockSpec(memory_space=pltpu.VMEM)
LIMIT = 60 * 1024 * 1024


def first_stage(g):
    return pl.pallas_call(
        first_kernel,
        out_shape=[jax.ShapeDtypeStruct((N, N), BF16)] * 2,
        in_specs=[VM],
        out_specs=[VM] * 2,
        scratch_shapes=[pltpu.VMEM((NB, N), F32)],
        compiler_params=pltpu.CompilerParams(vmem_limit_bytes=LIMIT),
        cost_estimate=pl.CostEstimate(flops=10**10, bytes_accessed=10**7, transcendentals=0),
        name="first_stage",
    )(g)


def second_stage(where, mine, theirs, w1h, w1l):
    return pl.pallas_call(
        second_kernel,
        out_shape=[jax.ShapeDtypeStruct((N, N), BF16)] * 4,
        in_specs=[pl.BlockSpec(memory_space=pltpu.SMEM)] + [VM] * 4,
        out_specs=[VM] * 4,
        scratch_shapes=[pltpu.VMEM((N, N), BF16)] * 2
        + [pltpu.VMEM((N, N), F32)]
        + [pltpu.VMEM((NB, N), F32)]
        + [pltpu.VMEM((N, N), BF16)] * 2,
        compiler_params=pltpu.CompilerParams(vmem_limit_bytes=LIMIT),
        cost_estimate=pl.CostEstimate(flops=2 * 10**10, bytes_accessed=10**7, transcendentals=0),
        name="second_stage",
    )(where, mine, theirs, w1h, w1l)


PER, GROUP = 2, 4
HALF = 256


def solve_tiles(src, w1h, w1l, w2h, w2l, gh, gl, put):
    KT = ((1,), (1,))
    p1 = jnp.concatenate([src[u, 0] for u in range(PER)], axis=0)
    p2 = jnp.concatenate([src[u, 1] for u in range(PER)], axis=0)
    parts = []
    for j in range(N // HALF):
        t, kk = slice(j * HALF, j * HALF + HALF), HALF * (j + 1)
        got = dot(p1[:, 0:kk], w1h[t, 0:kk], KT) + dot(p1[:, 0:kk], w1l[t, 0:kk], KT)
        parts.append(got.astype(BF16))
        put(j * HALF, parts[-1])
    l1 = jnp.concatenate(parts, axis=1)
    for j in range(N // HALF):
        t, kk = slice(j * HALF, j * HALF + HALF), HALF * (j + 1)
        got = dot(p2[:, 0:kk], w2h[t, 0:kk], KT) + dot(p2[:, 0:kk], w2l[t, 0:kk], KT)
        got = got + dot(l1, gh[t, :], KT) + dot(l1, gl[t, :], KT)
        put(N + j * HALF, got.astype(BF16))


def rows_kernel(need, own, src, w1h, w1l, w2h, w2l, gh, gl, own_first, own_second, out):
    step = pl.program_id(0)

    @pl.when(need[step] > 0)
    def _():
        def put(c, val):
            for u in range(PER):
                out[u, :, c : c + HALF] = val[u * HALF : u * HALF + HALF, :]

        solve_tiles(src, w1h, w1l, w2h, w2l, gh, gl, put)

    for u in range(PER):

        @pl.when(own[0] == step * PER + u)
        def _():
            own_first[0] = out[u, :, 0:N]
            own_second[0] = out[u, :, N : 2 * N]


ONCE = pl.BlockSpec((N, N), lambda s, *_: (0, 0), pipeline_mode=pl.Buffered(1))


def rows_stage(need, own, src, weights):
    count = src.shape[0]
    own_spec = pl.BlockSpec((1, HALF, N), lambda s, *_: (0, 0, 0))
    return pl.pallas_call(
        rows_kernel,
        out_shape=[
            jax.ShapeDtypeStruct((1, HALF, N), BF16),
            jax.ShapeDtypeStruct((1, HALF, N), BF16),
            jax.ShapeDtypeStruct((count, HALF, 2 * N), BF16),
        ],
        grid_spec=pltpu.PrefetchScalarGridSpec(
            num_scalar_prefetch=2,
            grid=(count // PER,),
            in_specs=[pl.BlockSpec((PER, 2, HALF, N), lambda s, *_: (s, 0, 0, 0))] + [ONCE] * 6,
            out_specs=[own_spec, own_spec, pl.BlockSpec((PER, HALF, 2 * N), lambda s, *_: (s, 0, 0))],
        ),
        compiler_params=pltpu.CompilerParams(vmem_limit_bytes=LIMIT, dimension_semantics=("arbitrary",)),
        cost_estimate=pl.CostEstimate(flops=4 * 10**10, bytes_accessed=4 * 10**7, transcendentals=0),
        name="rows_stage",
    )(need, own, src, *weights)


def final_kernel(pairs, live, need, src, w1h, w1l, w2h, w2l, gh, gl, rows, tin, tout, lcol, lrow, sem):
    KT = ((1,), (1,))
    step = pl.program_id(0)
    ncol = lcol.shape[0] // PER
    fetch = pltpu.make_async_copy(rows, lrow, sem)

    @pl.when(step == 0)
    def _():
        fetch.start()

    @pl.when(step < ncol)
    def _():
        at = jnp.minimum(step, ncol - 1)

        @pl.when(need[at] > 0)
        def _():
            def put(c, val):
                for u in range(PER):
                    lcol[at * PER + u, :, c : c + HALF] = val[u * HALF : u * HALF + HALF, :]

            solve_tiles(src, w1h, w1l, w2h, w2l, gh, gl, put)

    @pl.when(step == ncol)
    def _():
        fetch.wait()

    @pl.when(step >= ncol)
    def _():
        base = (step - ncol) * GROUP
        for u in range(GROUP):
            slot = base + u

            @pl.when(slot < live[0])
            def _():
                a, b = pairs[slot], pairs[24 + slot]
                tout[0, u] = tin[0, u] - dot(lrow[a], lcol[b], KT)

            @pl.when(slot >= live[0])
            def _():
                tout[0, u] = tin[0, u]


def final_stage(pairs, live, need, src, weights, rows, trailing):
    count, slots = src.shape[0], trailing.shape[1]
    cs, ks = count // PER, slots // GROUP
    tmap = lambda s, *_: (0, jnp.clip(s - cs, 0, ks - 1), 0, 0)
    return pl.pallas_call(
        final_kernel,
        out_shape=jax.ShapeDtypeStruct(trailing.shape, F32),
        grid_spec=pltpu.PrefetchScalarGridSpec(
            num_scalar_prefetch=3,
            grid=(cs + ks,),
            in_specs=[pl.BlockSpec((PER, 2, HALF, N), lambda s, *_: (jnp.minimum(s, cs - 1), 0, 0, 0))]
            + [ONCE] * 6
            + [pl.BlockSpec(memory_space=pl.ANY), pl.BlockSpec((1, GROUP, HALF, HALF), tmap)],
            out_specs=pl.BlockSpec((1, GROUP, HALF, HALF), tmap),
            scratch_shapes=[
                pltpu.VMEM((count, HALF, 2 * N), BF16),
                pltpu.VMEM(rows.shape, BF16),
                pltpu.SemaphoreType.DMA,
            ],
        ),
        compiler_params=pltpu.CompilerParams(vmem_limit_bytes=LIMIT, dimension_semantics=("arbitrary",)),
        cost_estimate=pl.CostEstimate(flops=3 * 10**10, bytes_accessed=4 * 10**7, transcendentals=0),
        name="final_stage",
    )(pairs, live, need, src, *weights, rows, trailing)


def spread(x, nrow, ncol):
    every = [(r, c) for r in range(nrow) for c in range(ncol)]
    half = ncol // 2
    flat = lambda r, c: r % nrow * ncol + c % ncol
    near, away = (
        lax.ppermute(x, ("row", "col"), [(flat(r, c + r + off), flat(r, c)) for r, c in every])
        for off in (0, half)
    )
    unit = jnp.stack([near, away], axis=0)
    up = lax.ppermute(unit, "row", [(r, (r + 2) % nrow) for r in range(nrow)])
    down = lax.ppermute(unit, "row", [(r, (r - 2) % nrow) for r in range(nrow)])
    row, col = lax.axis_index("row"), lax.axis_index("col")
    core = row % 2
    far = lax.ppermute(
        jnp.where(core == 0, up, down), "row", [(r, (r + (2 if r % 2 == 0 else -2)) % nrow) for r in range(nrow)]
    )
    mine = jnp.concatenate([unit, down, far, up], axis=0)
    theirs = lax.ppermute(mine, "row", [(r, r ^ 1) for r in range(nrow)])
    off = (jnp.arange(ncol, dtype=jnp.int32) - col) % ncol
    holder, side = off % half, off // half
    ahead = (holder // 2 - row // 2) % (nrow // 2)
    other = (holder % 2 != core).astype(jnp.int32)
    return mine, theirs, (other * mine.shape[0] + 2 * ahead + side).astype(jnp.int32)


def per_device(
    nrow, ncol, panel_first, panel_second, diag_first, bridge, diag_second, trailing, trail_pairs, live_count
):
    whole_first = lax.all_gather(diag_first, "col", axis=0, tiled=True)
    mine, theirs, where = spread(jnp.concatenate([bridge, diag_second], axis=0), nrow, ncol)
    both = jnp.stack([panel_first[0], panel_second[0]], axis=0)
    row_p = lax.all_gather(both, "col", axis=0)
    col_p = lax.all_gather(both, "row", axis=0)
    own = lax.axis_index("col").astype(jnp.int32)
    pairs = trail_pairs[0]
    active = jnp.arange(pairs.shape[1], dtype=jnp.int32) < live_count[0]
    group_r = jnp.arange(ncol // PER, dtype=jnp.int32)
    group_c = jnp.arange(nrow // PER, dtype=jnp.int32)
    need_row = jnp.any((pairs[0][None] // PER == group_r[:, None]) & active[None], axis=1) | (group_r == own // PER)
    need_col = jnp.any((pairs[1][None] // PER == group_c[:, None]) & active[None], axis=1)
    w1h, w1l = first_stage(whole_first)
    weights = (w1h, w1l, *second_stage(where, mine, theirs, w1h, w1l))
    lower_first, lower_second, rows = rows_stage(need_row.astype(jnp.int32), own[None], row_p, weights)
    owned = final_stage(pairs.reshape(-1), live_count, need_col.astype(jnp.int32), col_p, weights, rows, trailing)
    return lower_first, lower_second, owned


def solution(mesh):
    return jax.shard_map(
        functools.partial(per_device, mesh.shape["row"], mesh.shape["col"]),
        mesh=mesh,
        in_specs=(
            P(("row", "col"), None, None),
            P(("row", "col"), None, None),
            P("col", None),
            P("col", None),
            P("col", None),
            P(("row", "col"), None, None, None),
            P(("row", "col"), None, None),
            P(("row", "col")),
        ),
        out_specs=(
            P(("row", "col"), None, None),
            P(("row", "col"), None, None),
            P(("row", "col"), None, None, None),
        ),
        check_vma=False,
    )
```

```python
import functools

import jax
import jax.numpy as jnp
from jax import lax
from jax.experimental import pallas as pl
from jax.experimental.pallas import tpu as pltpu
from jax.sharding import PartitionSpec as P

F32, BF16 = jnp.float32, jnp.bfloat16
N, NB, Q = 1024, 128, 8


def split(x):
    hi = x.astype(BF16)
    return hi, (x - hi.astype(F32)).astype(BF16)


def dot(a, b, dims):
    return lax.dot_general(a, b, (dims, ((), ())), preferred_element_type=F32)


def diag_inverse(tiles, far_from=None):
    count = len(tiles)
    shape = (Q, NB)
    sub = lax.broadcasted_iota(jnp.int32, shape, 0)
    lane = lax.broadcasted_iota(jnp.int32, shape, 1)
    wide = lambda v: jnp.broadcast_to(v, shape)
    lanes = lambda v, c: jnp.take_along_axis(v, jnp.full(shape, c, jnp.int32), axis=1)
    zero = jnp.zeros(shape, F32)
    tiles = list(tiles)
    out = []

    def total(terms):
        while len(terms) > 1:
            terms = [a + b for a, b in zip(terms[::2], terms[1::2])] + ([terms[-1]] if len(terms) % 2 else [])
        return terms[0]

    def small(e):
        r, l, v = [], {}, {}
        for m in range(Q):
            rm = lax.rsqrt(e[m, m])
            r.append(rm)
            for i in range(m + 1, Q):
                l[i, m] = e[i, m] * rm
            for j in range(m + 1, Q):
                for i in range(j, Q):
                    e[i, j] = e[i, j] - l[i, m] * l[j, m]
            v[m, m] = rm
            for k in range(m):
                v[m, k] = -(rm * total([l[m, j] * v[j, k] for j in range(k, m)]))
        return v

    def assemble(coef):
        cols = []
        for k in range(Q):
            col = zero
            for i in range(Q):
                got = coef(i, k)
                if got is not None:
                    col = jnp.where(sub == i, got, col)
            cols.append(col)
        return cols

    def spread_rows(x):
        return [wide(x[k : k + 1, :]) for k in range(Q)]

    def apply(cols, rows):
        return total([c * x for c, x in zip(cols, rows)])

    for s in range(0, count, 2):
        c0, c1 = Q * s, Q * s + Q
        b0, b1 = tiles[s], tiles[s + 1]
        in0 = (lane >= c0) & (lane < c1)
        in1 = (lane >= c1) & (lane < c1 + Q)
        d0 = [lanes(b0, c0 + m) for m in range(Q)]
        a = [lanes(b1, c0 + m) for m in range(Q)]
        d1 = [lanes(b1, c1 + m) for m in range(Q)]
        v0 = small({(i, m): wide(d0[m][i : i + 1, :]) for m in range(Q) for i in range(m, Q)})
        q, qs = [], []
        for k in range(Q):
            qk = total([a[j] * v0[k, j] for j in range(k + 1)])
            q.append(qk)
            qs.append(spread_rows(qk))
        for m in range(Q):
            d1[m] = d1[m] - total([q[k] * qs[k][m] for k in range(Q)])
        v1 = small({(i, m): wide(d1[m][i : i + 1, :]) for m in range(Q) for i in range(m, Q)})
        t0 = jnp.where(in0, jnp.where(lane - c0 == sub, 1.0, 0.0), jnp.where(in1, 0.0, b0))
        v0t = assemble(lambda i, k: v0[k, i] if i <= k else None)
        w0 = apply(assemble(lambda i, k: v0[i, k] if i >= k else None), spread_rows(t0))
        w0r = spread_rows(w0)
        out.append(jnp.where(lane < c1, w0, 0.0))
        t1 = jnp.where(in0, 0.0, b1) - total([q[k] * w0r[k] for k in range(Q)])
        t1 = jnp.where(in1, jnp.where(lane - c1 == sub, 1.0, 0.0), t1)
        w1 = apply(assemble(lambda i, k: v1[i, k] if i >= k else None), spread_rows(t1))
        out.append(jnp.where(lane < c1 + Q, w1, 0.0))
        if s + 2 < count:
            w1r = spread_rows(w1)
            z1 = apply(assemble(lambda i, k: v1[k, i] if i <= k else None), w1r)
            z1r = spread_rows(z1)
            y = w0 - apply(assemble(lambda i, k: qs[i][k]), z1r)
            zr = spread_rows(apply(v0t, spread_rows(y))) + z1r
            both = in0 | in1
            for t in range(s + 2, count):
                row = tiles[t]
                terms = [lanes(row, c0 + m) * zr[m] for m in range(2 * Q)]
                tiles[t] = jnp.where(both, 0.0, row) - total(terms)
    return out


def factor(load_row, rh, rl, tri, start=None):
    blocks = N // NB
    lane = lax.broadcasted_iota(jnp.int32, (NB, N), 1)
    K0 = ((0,), (0,))
    KM = ((1,), (0,))

    rh[...] = jnp.zeros((N, N), BF16)
    rl[...] = jnp.zeros((N, N), BF16)

    def step(k, carry):
        k0 = pl.multiple_of(k * NB, NB)
        tri[...] = jnp.where(lane >= k0, load_row(k0), 0.0)
        cols = pl.ds(k0, NB)

        def update(p, c):
            rows = pl.ds(pl.multiple_of(p * 2 * NB, 2 * NB), 2 * NB)
            ah, al = rh[rows, cols], rl[rows, cols]
            bh, bl = rh[rows, :], rl[rows, :]
            tri[...] -= dot(ah, bh, K0) + dot(ah, bl, K0) + dot(al, bh, K0)
            return c

        lax.fori_loop(0, (k + 1) // 2, update, 0)
        rh[:, cols] = jnp.zeros((N, NB), BF16)
        rl[:, cols] = jnp.zeros((N, NB), BF16)
        d = tri[:, pl.ds(k0, NB)]
        tiles = diag_inverse([d[Q * i : Q * i + Q, :] for i in range(NB // Q)])
        w = jnp.concatenate(tiles, axis=0)
        tri[:, pl.ds(k0, NB)] = jnp.eye(NB, dtype=F32)
        wh, wl = split(w)
        xh, xl = split(tri[...])
        row = dot(wh, xh, KM) + dot(wh, xl, KM) + dot(wl, xh, KM)
        oh, ol = split(row)
        rh[pl.ds(k0, NB), :] = oh
        rl[pl.ds(k0, NB), :] = ol
        return carry

    lax.fori_loop(0, blocks, step, 0)


def first_kernel(g_ref, oh, ol, tri):
    def load(k0):
        return g_ref[pl.ds(k0, NB), :].astype(F32)

    factor(load, oh, ol, tri)


def second_kernel(where, mine, theirs, w1h, w1l, oh, ol, gh, gl, ch, cl, shifted, tri, bridge, diag):
    KT = ((1,), (1,))
    KM = ((1,), (0,))
    half = 256
    shard = N // where.shape[0]
    for i in range(where.shape[0]):
        at = where[i]
        rows = slice(i * shard, i * shard + shard)
        for base, ref in ((0, mine), (mine.shape[0], theirs)):

            @pl.when((at >= base) & (at < base + ref.shape[0]))
            def _():
                got = ref[jnp.clip(at - base, 0, ref.shape[0] - 1)]
                bridge[rows, :] = got[0:shard]
                diag[rows, :] = got[shard : 2 * shard]

    def couple(i, c):
        rows = pl.ds(pl.multiple_of(i * 2 * half, 2 * half), 2 * half)
        for j in range(N // half):
            t, kk = slice(j * half, j * half + half), half * (j + 1)
            b = bridge[rows, 0:kk]
            hi, lo = split(dot(b, w1h[t, 0:kk], KT) + dot(b, w1l[t, 0:kk], KT))
            ch[rows, t] = hi
            cl[rows, t] = lo
        return c

    lax.fori_loop(0, N // (2 * half), couple, 0)

    def shift(i, c):
        s = pl.ds(pl.multiple_of(i * half, half), half)

        def inner(j, c):
            t = pl.ds(pl.multiple_of(j * half, half), half)
            prod = dot(ch[s, :], ch[t, :], KT) + dot(ch[s, :], cl[t, :], KT) + dot(cl[s, :], ch[t, :], KT)
            shifted[s, t] = diag[s, t].astype(F32) - prod
            return c

        return lax.fori_loop(i, N // half, inner, c)

    lax.fori_loop(0, N // half, shift, 0)
    factor(lambda k0: shifted[pl.ds(k0, NB), :], oh, ol, tri)

    def carry_over(j, c):
        t = pl.ds(pl.multiple_of(j * 2 * half, 2 * half), 2 * half)
        for i in range(N // half):
            s, kk = slice(i * half, i * half + half), half * (i + 1)
            hi, lo = split(
                -(
                    dot(oh[s, 0:kk], ch[0:kk, t], KM)
                    + dot(oh[s, 0:kk], cl[0:kk, t], KM)
                    + dot(ol[s, 0:kk], ch[0:kk, t], KM)
                )
            )
            gh[s, t] = hi
            gl[s, t] = lo
        return c

    lax.fori_loop(0, N // (2 * half), carry_over, 0)


VM = pl.BlockSpec(memory_space=pltpu.VMEM)
LIMIT = 60 * 1024 * 1024


def first_stage(g):
    return pl.pallas_call(
        first_kernel,
        out_shape=[jax.ShapeDtypeStruct((N, N), BF16)] * 2,
        in_specs=[VM],
        out_specs=[VM] * 2,
        scratch_shapes=[pltpu.VMEM((NB, N), F32)],
        compiler_params=pltpu.CompilerParams(vmem_limit_bytes=LIMIT),
        cost_estimate=pl.CostEstimate(flops=10**10, bytes_accessed=10**7, transcendentals=0),
        name="first_stage",
    )(g)


def second_stage(where, mine, theirs, w1h, w1l):
    return pl.pallas_call(
        second_kernel,
        out_shape=[jax.ShapeDtypeStruct((N, N), BF16)] * 4,
        in_specs=[pl.BlockSpec(memory_space=pltpu.SMEM)] + [VM] * 4,
        out_specs=[VM] * 4,
        scratch_shapes=[pltpu.VMEM((N, N), BF16)] * 2
        + [pltpu.VMEM((N, N), F32)]
        + [pltpu.VMEM((NB, N), F32)]
        + [pltpu.VMEM((N, N), BF16)] * 2,
        compiler_params=pltpu.CompilerParams(vmem_limit_bytes=LIMIT),
        cost_estimate=pl.CostEstimate(flops=2 * 10**10, bytes_accessed=10**7, transcendentals=0),
        name="second_stage",
    )(where, mine, theirs, w1h, w1l)


PER, GROUP, SLOTS = 2, 4, 24
HALF = 256


def solve_tiles(src, w1h, w1l, w2h, w2l, gh, gl, put):
    KT = ((1,), (1,))
    p1 = jnp.concatenate([src[u, 0] for u in range(PER)], axis=0)
    p2 = jnp.concatenate([src[u, 1] for u in range(PER)], axis=0)
    parts = []
    for j in range(N // HALF):
        t, kk = slice(j * HALF, j * HALF + HALF), HALF * (j + 1)
        got = dot(p1[:, 0:kk], w1h[t, 0:kk], KT) + dot(p1[:, 0:kk], w1l[t, 0:kk], KT)
        parts.append(got.astype(BF16))
        put(j * HALF, parts[-1])
    l1 = jnp.concatenate(parts, axis=1)
    for j in range(N // HALF):
        t, kk = slice(j * HALF, j * HALF + HALF), HALF * (j + 1)
        got = dot(p2[:, 0:kk], w2h[t, 0:kk], KT) + dot(p2[:, 0:kk], w2l[t, 0:kk], KT)
        got = got + dot(l1, gh[t, :], KT) + dot(l1, gl[t, :], KT)
        put(N + j * HALF, got.astype(BF16))


ONCE = pl.BlockSpec((N, N), lambda s, *_: (0, 0), pipeline_mode=pl.Buffered(1))
ANY = pl.BlockSpec(memory_space=pl.ANY)


def put_into(ref, base):
    def put(c, val):
        for u in range(PER):
            ref[base + u, :, c : c + HALF] = val[u * HALF : u * HALF + HALF, :]

    return put


def cols_kernel(a0, a1, a2, a3, w1h, w1l, w2h, w2l, gh, gl, own_first, own_second, out, buf, sems):
    step = pl.program_id(0)
    copies = [pltpu.make_async_copy(a, buf.at[i], sems.at[i]) for i, a in enumerate((a0, a1, a2, a3))]

    @pl.when(step == 0)
    def _():
        for copy in copies:
            copy.start()
        for copy in copies[:PER]:
            copy.wait()

    @pl.when(step == 1)
    def _():
        for copy in copies[PER:]:
            copy.wait()

    solve_tiles(buf.at[pl.ds(step * PER, PER)], w1h, w1l, w2h, w2l, gh, gl, put_into(out, 0))

    @pl.when(step == 0)
    def _():
        own_first[0] = out[0, :, 0:N]
        own_second[0] = out[0, :, N : 2 * N]


def cols_stage(arrays, weights):
    count = len(arrays)
    own_spec = pl.BlockSpec((1, HALF, N), lambda s, *_: (0, 0, 0))
    return pl.pallas_call(
        cols_kernel,
        out_shape=[
            jax.ShapeDtypeStruct((1, HALF, N), BF16),
            jax.ShapeDtypeStruct((1, HALF, N), BF16),
            jax.ShapeDtypeStruct((count, HALF, 2 * N), BF16),
        ],
        grid=(count // PER,),
        in_specs=[ANY] * count + [ONCE] * 6,
        out_specs=[own_spec, own_spec, pl.BlockSpec((PER, HALF, 2 * N), lambda s: (s, 0, 0))],
        scratch_shapes=[pltpu.VMEM((count, 2, HALF, N), BF16), pltpu.SemaphoreType.DMA((count,))],
        compiler_params=pltpu.CompilerParams(vmem_limit_bytes=LIMIT, dimension_semantics=("arbitrary",)),
        cost_estimate=pl.CostEstimate(flops=10**10, bytes_accessed=3 * 10**7, transcendentals=0),
        name="cols_stage",
    )(*arrays, *weights)


def rows_kernel(need, src, w1h, w1l, w2h, w2l, gh, gl, out):
    @pl.when(need[pl.program_id(0)] > 0)
    def _():
        solve_tiles(src, w1h, w1l, w2h, w2l, gh, gl, put_into(out, 0))


def rows_stage(need, src, weights):
    count = src.shape[0] // 2
    return pl.pallas_call(
        rows_kernel,
        out_shape=jax.ShapeDtypeStruct((count, HALF, 2 * N), BF16),
        grid_spec=pltpu.PrefetchScalarGridSpec(
            num_scalar_prefetch=1,
            grid=(count // PER,),
            in_specs=[pl.BlockSpec((PER, 2, HALF, N), lambda s, *_: (s, 0, 0, 0))] + [ONCE] * 6,
            out_specs=pl.BlockSpec((PER, HALF, 2 * N), lambda s, *_: (s, 0, 0)),
        ),
        compiler_params=pltpu.CompilerParams(vmem_limit_bytes=LIMIT, dimension_semantics=("arbitrary",)),
        cost_estimate=pl.CostEstimate(flops=2 * 10**10, bytes_accessed=4 * 10**7, transcendentals=0),
        name="rows_stage",
    )(need, src, *weights)


def final_kernel(
    pairs, live, need, src, w1h, w1l, w2h, w2l, gh, gl, done_rows, mine, theirs, tin, tout, lcol, lrow, sems
):
    KT = ((1,), (1,))
    step = pl.program_id(0)
    first, side = done_rows.shape[0], mine.shape[0]
    steps = (lrow.shape[0] - first) // PER
    copies = [
        pltpu.make_async_copy(done_rows, lrow.at[pl.ds(0, first)], sems.at[0]),
        pltpu.make_async_copy(mine, lcol.at[pl.ds(0, side)], sems.at[1]),
        pltpu.make_async_copy(theirs, lcol.at[pl.ds(side, side)], sems.at[2]),
    ]

    @pl.when(step == 0)
    def _():
        for copy in copies:
            copy.start()

    @pl.when(step < steps)
    def _():
        at = jnp.minimum(step, steps - 1)

        @pl.when(need[steps + at] > 0)
        def _():
            solve_tiles(src, w1h, w1l, w2h, w2l, gh, gl, put_into(lrow, first + at * PER))

    @pl.when(step == steps)
    def _():
        for copy in copies:
            copy.wait()

    @pl.when(step >= steps)
    def _():
        base = (step - steps) * GROUP
        for u in range(GROUP):
            slot = base + u

            @pl.when(slot < live[0])
            def _():
                a, b = pairs[slot], pairs[SLOTS + slot]
                tout[0, u] = tin[0, u] - dot(lrow[a], lcol[b], KT)

            @pl.when(slot >= live[0])
            def _():
                tout[0, u] = tin[0, u]


def final_stage(pairs, live, need, src, weights, done_rows, mine, theirs, trailing):
    count, slots = src.shape[0], trailing.shape[1]
    cs, ks = done_rows.shape[0] // PER, slots // GROUP
    tmap = lambda s, *_: (0, jnp.clip(s - cs, 0, ks - 1), 0, 0)
    return pl.pallas_call(
        final_kernel,
        out_shape=jax.ShapeDtypeStruct(trailing.shape, F32),
        grid_spec=pltpu.PrefetchScalarGridSpec(
            num_scalar_prefetch=3,
            grid=(cs + ks,),
            in_specs=[pl.BlockSpec((PER, 2, HALF, N), lambda s, *_: (cs + jnp.minimum(s, cs - 1), 0, 0, 0))]
            + [ONCE] * 6
            + [ANY] * 3
            + [pl.BlockSpec((1, GROUP, HALF, HALF), tmap)],
            out_specs=pl.BlockSpec((1, GROUP, HALF, HALF), tmap),
            scratch_shapes=[
                pltpu.VMEM((2 * mine.shape[0], HALF, 2 * N), BF16),
                pltpu.VMEM((count, HALF, 2 * N), BF16),
                pltpu.SemaphoreType.DMA((3,)),
            ],
        ),
        compiler_params=pltpu.CompilerParams(vmem_limit_bytes=LIMIT, dimension_semantics=("arbitrary",)),
        cost_estimate=pl.CostEstimate(flops=3 * 10**10, bytes_accessed=4 * 10**7, transcendentals=0),
        name="final_stage",
    )(pairs, live, need, src, *weights, done_rows, mine, theirs, trailing)


def spread(x, nrow, ncol):
    every = [(r, c) for r in range(nrow) for c in range(ncol)]
    half = ncol // 2
    flat = lambda r, c: r % nrow * ncol + c % ncol
    near, away = (
        lax.ppermute(x, ("row", "col"), [(flat(r, c + r + off), flat(r, c)) for r, c in every])
        for off in (0, half)
    )
    unit = jnp.stack([near, away], axis=0)
    up = lax.ppermute(unit, "row", [(r, (r + 2) % nrow) for r in range(nrow)])
    down = lax.ppermute(unit, "row", [(r, (r - 2) % nrow) for r in range(nrow)])
    row, col = lax.axis_index("row"), lax.axis_index("col")
    core = row % 2
    far = lax.ppermute(
        jnp.where(core == 0, up, down), "row", [(r, (r + (2 if r % 2 == 0 else -2)) % nrow) for r in range(nrow)]
    )
    mine = jnp.concatenate([unit, down, far, up], axis=0)
    theirs = lax.ppermute(mine, "row", [(r, r ^ 1) for r in range(nrow)])
    off = (jnp.arange(ncol, dtype=jnp.int32) - col) % ncol
    holder, side = off % half, off // half
    ahead = (holder // 2 - row // 2) % (nrow // 2)
    other = (holder % 2 != core).astype(jnp.int32)
    return mine, theirs, (other * mine.shape[0] + 2 * ahead + side).astype(jnp.int32)


def per_device(
    nrow, ncol, panel_first, panel_second, diag_first, bridge, diag_second, trailing, trail_pairs, live_count
):
    whole_first = lax.all_gather(diag_first, "col", axis=0, tiled=True)
    mine, theirs, where = spread(jnp.concatenate([bridge, diag_second], axis=0), nrow, ncol)
    both = jnp.stack([panel_first[0], panel_second[0]], axis=0)
    row_p = lax.all_gather(both, "col", axis=0)
    held, mine = lax.optimization_barrier((both, mine))
    up, down, far = (
        lax.ppermute(held, "row", [(r, (r + d) % nrow) for r in range(nrow)]) for d in (2, -2, nrow // 2)
    )
    row = lax.axis_index("row")
    pairs = trail_pairs[0]
    seat = 4 * (pairs[1] % 2 != row % 2).astype(jnp.int32) + (pairs[1] // 2 - row // 2) % (nrow // 2)
    active = jnp.arange(pairs.shape[1], dtype=jnp.int32) < live_count[0]
    group = jnp.arange(ncol // PER, dtype=jnp.int32)
    need = jnp.any((pairs[0][None] // PER == group[:, None]) & active[None], axis=1).astype(jnp.int32)
    w1h, w1l = first_stage(whole_first)
    weights = (w1h, w1l, *second_stage(where, mine, theirs, w1h, w1l))
    lower_first, lower_second, ours = cols_stage((held, down, far, up), weights)
    others = lax.ppermute(ours, "row", [(r, r ^ 1) for r in range(nrow)])
    done_rows = rows_stage(need, row_p, weights)
    owned = final_stage(
        jnp.concatenate([pairs[0], seat]).astype(jnp.int32), live_count, need, row_p, weights, done_rows, ours, others, trailing
    )
    return lower_first, lower_second, owned


def solution(mesh):
    return jax.shard_map(
        functools.partial(per_device, mesh.shape["row"], mesh.shape["col"]),
        mesh=mesh,
        in_specs=(
            P(("row", "col"), None, None),
            P(("row", "col"), None, None),
            P("col", None),
            P("col", None),
            P("col", None),
            P(("row", "col"), None, None, None),
            P(("row", "col"), None, None),
            P(("row", "col")),
        ),
        out_specs=(
            P(("row", "col"), None, None),
            P(("row", "col"), None, None),
            P(("row", "col"), None, None, None),
        ),
        check_vma=False,
    )
```

```python
import functools

import jax
import jax.numpy as jnp
from jax import lax
from jax.experimental import pallas as pl
from jax.experimental.pallas import tpu as pltpu
from jax.sharding import PartitionSpec as P

F32, BF16 = jnp.float32, jnp.bfloat16
N, NB, Q = 1024, 128, 8


def split(x):
    hi = x.astype(BF16)
    return hi, (x - hi.astype(F32)).astype(BF16)


def dot(a, b, dims):
    return lax.dot_general(a, b, (dims, ((), ())), preferred_element_type=F32)


def diag_inverse(tiles, far_from=None):
    count = len(tiles)
    shape = (Q, NB)
    sub = lax.broadcasted_iota(jnp.int32, shape, 0)
    lane = lax.broadcasted_iota(jnp.int32, shape, 1)
    wide = lambda v: jnp.broadcast_to(v, shape)
    lanes = lambda v, c: jnp.take_along_axis(v, jnp.full(shape, c, jnp.int32), axis=1)
    zero = jnp.zeros(shape, F32)
    tiles = list(tiles)
    out = []

    def total(terms):
        while len(terms) > 1:
            terms = [a + b for a, b in zip(terms[::2], terms[1::2])] + ([terms[-1]] if len(terms) % 2 else [])
        return terms[0]

    def small(e):
        r, l, v = [], {}, {}
        for m in range(Q):
            rm = lax.rsqrt(e[m, m])
            r.append(rm)
            for i in range(m + 1, Q):
                l[i, m] = e[i, m] * rm
            for j in range(m + 1, Q):
                for i in range(j, Q):
                    e[i, j] = e[i, j] - l[i, m] * l[j, m]
            v[m, m] = rm
            for k in range(m):
                v[m, k] = -(rm * total([l[m, j] * v[j, k] for j in range(k, m)]))
        return v

    def assemble(coef):
        cols = []
        for k in range(Q):
            col = zero
            for i in range(Q):
                got = coef(i, k)
                if got is not None:
                    col = jnp.where(sub == i, got, col)
            cols.append(col)
        return cols

    def spread_rows(x):
        return [wide(x[k : k + 1, :]) for k in range(Q)]

    def apply(cols, rows):
        return total([c * x for c, x in zip(cols, rows)])

    for s in range(0, count, 2):
        c0, c1 = Q * s, Q * s + Q
        b0, b1 = tiles[s], tiles[s + 1]
        in0 = (lane >= c0) & (lane < c1)
        in1 = (lane >= c1) & (lane < c1 + Q)
        d0 = [lanes(b0, c0 + m) for m in range(Q)]
        a = [lanes(b1, c0 + m) for m in range(Q)]
        d1 = [lanes(b1, c1 + m) for m in range(Q)]
        v0 = small({(i, m): wide(d0[m][i : i + 1, :]) for m in range(Q) for i in range(m, Q)})
        q, qs = [], []
        for k in range(Q):
            qk = total([a[j] * v0[k, j] for j in range(k + 1)])
            q.append(qk)
            qs.append(spread_rows(qk))
        for m in range(Q):
            d1[m] = d1[m] - total([q[k] * qs[k][m] for k in range(Q)])
        v1 = small({(i, m): wide(d1[m][i : i + 1, :]) for m in range(Q) for i in range(m, Q)})
        t0 = jnp.where(in0, jnp.where(lane - c0 == sub, 1.0, 0.0), jnp.where(in1, 0.0, b0))
        v0t = assemble(lambda i, k: v0[k, i] if i <= k else None)
        w0 = apply(assemble(lambda i, k: v0[i, k] if i >= k else None), spread_rows(t0))
        w0r = spread_rows(w0)
        out.append(jnp.where(lane < c1, w0, 0.0))
        t1 = jnp.where(in0, 0.0, b1) - total([q[k] * w0r[k] for k in range(Q)])
        t1 = jnp.where(in1, jnp.where(lane - c1 == sub, 1.0, 0.0), t1)
        w1 = apply(assemble(lambda i, k: v1[i, k] if i >= k else None), spread_rows(t1))
        out.append(jnp.where(lane < c1 + Q, w1, 0.0))
        if s + 2 < count:
            w1r = spread_rows(w1)
            z1 = apply(assemble(lambda i, k: v1[k, i] if i <= k else None), w1r)
            z1r = spread_rows(z1)
            y = w0 - apply(assemble(lambda i, k: qs[i][k]), z1r)
            z0 = apply(v0t, spread_rows(y))
            zr = spread_rows(z0) + z1r
            both = in0 | in1
            if s + 4 < count:
                lhs = jnp.concatenate([b0, b1], axis=0)[:, Q * (s + 4) :]
                rhs = jnp.concatenate([z0, z1], axis=0)
                away = lax.dot_general(lhs, rhs, (((0,), (0,)), ((), ())), precision=lax.Precision.HIGHEST, preferred_element_type=F32)
                for t in range(s + 4, count):
                    tiles[t] = jnp.where(both, 0.0, tiles[t]) - away[Q * (t - s - 4) : Q * (t - s - 3), :]
            for t in range(s + 2, min(s + 4, count)):
                row = tiles[t]
                terms = [lanes(row, c0 + m) * zr[m] for m in range(2 * Q)]
                tiles[t] = jnp.where(both, 0.0, row) - total(terms)
    return out


def factor(load_row, rh, rl, tri, start=None):
    blocks = N // NB
    lane = lax.broadcasted_iota(jnp.int32, (NB, N), 1)
    K0 = ((0,), (0,))
    KM = ((1,), (0,))

    rh[...] = jnp.zeros((N, N), BF16)
    rl[...] = jnp.zeros((N, N), BF16)

    def step(k, carry):
        k0 = pl.multiple_of(k * NB, NB)
        tri[...] = jnp.where(lane >= k0, load_row(k0), 0.0)
        cols = pl.ds(k0, NB)

        def update(p, c):
            rows = pl.ds(pl.multiple_of(p * 2 * NB, 2 * NB), 2 * NB)
            ah, al = rh[rows, cols], rl[rows, cols]
            bh, bl = rh[rows, :], rl[rows, :]
            pair = dot(jnp.concatenate([ah, al], axis=1), bh, K0)
            tri[...] -= pair[0:NB] + pair[NB:] + dot(ah, bl, K0)
            return c

        lax.fori_loop(0, (k + 1) // 2, update, 0)
        rh[:, cols] = jnp.zeros((N, NB), BF16)
        rl[:, cols] = jnp.zeros((N, NB), BF16)
        d = tri[:, pl.ds(k0, NB)]
        tiles = diag_inverse([d[Q * i : Q * i + Q, :] for i in range(NB // Q)])
        w = jnp.concatenate(tiles, axis=0)
        tri[:, pl.ds(k0, NB)] = jnp.eye(NB, dtype=F32)
        wh, wl = split(w)
        xh, xl = split(tri[...])
        pair = dot(jnp.concatenate([wh, wl], axis=0), xh, KM)
        row = pair[0:NB] + pair[NB:] + dot(wh, xl, KM)
        oh, ol = split(row)
        rh[pl.ds(k0, NB), :] = oh
        rl[pl.ds(k0, NB), :] = ol
        return carry

    lax.fori_loop(0, blocks, step, 0)


def first_kernel(g_ref, oh, ol, tri):
    def load(k0):
        return g_ref[pl.ds(k0, NB), :].astype(F32)

    factor(load, oh, ol, tri)


def second_kernel(where, mine, theirs, w1h, w1l, oh, ol, gh, gl, ch, cl, shifted, tri, bridge, diag):
    KT = ((1,), (1,))
    KM = ((1,), (0,))
    half = 256
    shard = N // where.shape[0]
    for i in range(where.shape[0]):
        at = where[i]
        rows = slice(i * shard, i * shard + shard)
        for base, ref in ((0, mine), (mine.shape[0], theirs)):

            @pl.when((at >= base) & (at < base + ref.shape[0]))
            def _():
                got = ref[jnp.clip(at - base, 0, ref.shape[0] - 1)]
                bridge[rows, :] = got[0:shard]
                diag[rows, :] = got[shard : 2 * shard]

    def couple(i, c):
        rows = pl.ds(pl.multiple_of(i * 2 * half, 2 * half), 2 * half)
        for j in range(N // half):
            t, kk = slice(j * half, j * half + half), half * (j + 1)
            b = bridge[rows, 0:kk]
            hi, lo = split(dot(b, w1h[t, 0:kk], KT) + dot(b, w1l[t, 0:kk], KT))
            ch[rows, t] = hi
            cl[rows, t] = lo
        return c

    lax.fori_loop(0, N // (2 * half), couple, 0)

    def shift(i, c):
        s = pl.ds(pl.multiple_of(i * half, half), half)

        def inner(j, c):
            t = pl.ds(pl.multiple_of(j * half, half), half)
            pair = dot(jnp.concatenate([ch[s, :], cl[s, :]], axis=0), ch[t, :], KT)
            prod = pair[0:half] + pair[half:] + dot(ch[s, :], cl[t, :], KT)
            shifted[s, t] = diag[s, t].astype(F32) - prod
            return c

        return lax.fori_loop(i, N // half, inner, c)

    lax.fori_loop(0, N // half, shift, 0)
    factor(lambda k0: shifted[pl.ds(k0, NB), :], oh, ol, tri)

    def carry_over(j, c):
        t = pl.ds(pl.multiple_of(j * 2 * half, 2 * half), 2 * half)
        for i in range(N // half):
            s, kk = slice(i * half, i * half + half), half * (i + 1)
            hi, lo = split(
                -(
                    dot(oh[s, 0:kk], ch[0:kk, t], KM)
                    + dot(oh[s, 0:kk], cl[0:kk, t], KM)
                    + dot(ol[s, 0:kk], ch[0:kk, t], KM)
                )
            )
            gh[s, t] = hi
            gl[s, t] = lo
        return c

    lax.fori_loop(0, N // (2 * half), carry_over, 0)


VM = pl.BlockSpec(memory_space=pltpu.VMEM)
LIMIT = 60 * 1024 * 1024


def first_stage(g):
    return pl.pallas_call(
        first_kernel,
        out_shape=[jax.ShapeDtypeStruct((N, N), BF16)] * 2,
        in_specs=[VM],
        out_specs=[VM] * 2,
        scratch_shapes=[pltpu.VMEM((NB, N), F32)],
        compiler_params=pltpu.CompilerParams(vmem_limit_bytes=LIMIT),
        cost_estimate=pl.CostEstimate(flops=10**10, bytes_accessed=10**7, transcendentals=0),
        name="first_stage",
    )(g)


def second_stage(where, mine, theirs, w1h, w1l):
    return pl.pallas_call(
        second_kernel,
        out_shape=[jax.ShapeDtypeStruct((N, N), BF16)] * 4,
        in_specs=[pl.BlockSpec(memory_space=pltpu.SMEM)] + [VM] * 4,
        out_specs=[VM] * 4,
        scratch_shapes=[pltpu.VMEM((N, N), BF16)] * 2
        + [pltpu.VMEM((N, N), F32)]
        + [pltpu.VMEM((NB, N), F32)]
        + [pltpu.VMEM((N, N), BF16)] * 2,
        compiler_params=pltpu.CompilerParams(vmem_limit_bytes=LIMIT),
        cost_estimate=pl.CostEstimate(flops=2 * 10**10, bytes_accessed=10**7, transcendentals=0),
        name="second_stage",
    )(where, mine, theirs, w1h, w1l)


PER, GROUP, SLOTS = 2, 4, 24
HALF = 256


def solve_tiles(src, w1h, w1l, w2h, w2l, gh, gl, put):
    KT = ((1,), (1,))
    p1 = jnp.concatenate([src[u, 0] for u in range(PER)], axis=0)
    p2 = jnp.concatenate([src[u, 1] for u in range(PER)], axis=0)
    parts = []
    for j in range(N // HALF):
        t, kk = slice(j * HALF, j * HALF + HALF), HALF * (j + 1)
        got = dot(p1[:, 0:kk], w1h[t, 0:kk], KT) + dot(p1[:, 0:kk], w1l[t, 0:kk], KT)
        parts.append(got.astype(BF16))
        put(j * HALF, parts[-1])
    l1 = jnp.concatenate(parts, axis=1)
    for j in range(N // HALF):
        t, kk = slice(j * HALF, j * HALF + HALF), HALF * (j + 1)
        got = dot(p2[:, 0:kk], w2h[t, 0:kk], KT) + dot(p2[:, 0:kk], w2l[t, 0:kk], KT)
        got = got + dot(l1, gh[t, :], KT) + dot(l1, gl[t, :], KT)
        put(N + j * HALF, got.astype(BF16))


ONCE = pl.BlockSpec((N, N), lambda s, *_: (0, 0), pipeline_mode=pl.Buffered(1))
ANY = pl.BlockSpec(memory_space=pl.ANY)


def put_into(ref, base):
    def put(c, val):
        for u in range(PER):
            ref[base + u, :, c : c + HALF] = val[u * HALF : u * HALF + HALF, :]

    return put


def cols_kernel(a0, a1, a2, a3, w1h, w1l, w2h, w2l, gh, gl, own_first, own_second, out, buf, sems):
    step = pl.program_id(0)
    copies = [pltpu.make_async_copy(a, buf.at[i], sems.at[i]) for i, a in enumerate((a0, a1, a2, a3))]

    @pl.when(step == 0)
    def _():
        for copy in copies:
            copy.start()
        for copy in copies[:PER]:
            copy.wait()

    @pl.when(step == 1)
    def _():
        for copy in copies[PER:]:
            copy.wait()

    solve_tiles(buf.at[pl.ds(step * PER, PER)], w1h, w1l, w2h, w2l, gh, gl, put_into(out, 0))

    @pl.when(step == 0)
    def _():
        own_first[0] = out[0, :, 0:N]
        own_second[0] = out[0, :, N : 2 * N]


def cols_stage(arrays, weights):
    count = len(arrays)
    own_spec = pl.BlockSpec((1, HALF, N), lambda s, *_: (0, 0, 0))
    return pl.pallas_call(
        cols_kernel,
        out_shape=[
            jax.ShapeDtypeStruct((1, HALF, N), BF16),
            jax.ShapeDtypeStruct((1, HALF, N), BF16),
            jax.ShapeDtypeStruct((count, HALF, 2 * N), BF16),
        ],
        grid=(count // PER,),
        in_specs=[ANY] * count + [ONCE] * 6,
        out_specs=[own_spec, own_spec, pl.BlockSpec((PER, HALF, 2 * N), lambda s: (s, 0, 0))],
        scratch_shapes=[pltpu.VMEM((count, 2, HALF, N), BF16), pltpu.SemaphoreType.DMA((count,))],
        compiler_params=pltpu.CompilerParams(vmem_limit_bytes=LIMIT, dimension_semantics=("arbitrary",)),
        cost_estimate=pl.CostEstimate(flops=10**10, bytes_accessed=3 * 10**7, transcendentals=0),
        name="cols_stage",
    )(*arrays, *weights)


def rows_kernel(need, src, w1h, w1l, w2h, w2l, gh, gl, out):
    @pl.when(need[pl.program_id(0)] > 0)
    def _():
        solve_tiles(src, w1h, w1l, w2h, w2l, gh, gl, put_into(out, 0))


def rows_stage(need, src, weights):
    count = src.shape[0] // 2
    return pl.pallas_call(
        rows_kernel,
        out_shape=jax.ShapeDtypeStruct((count, HALF, 2 * N), BF16),
        grid_spec=pltpu.PrefetchScalarGridSpec(
            num_scalar_prefetch=1,
            grid=(count // PER,),
            in_specs=[pl.BlockSpec((PER, 2, HALF, N), lambda s, *_: (s, 0, 0, 0))] + [ONCE] * 6,
            out_specs=pl.BlockSpec((PER, HALF, 2 * N), lambda s, *_: (s, 0, 0)),
        ),
        compiler_params=pltpu.CompilerParams(vmem_limit_bytes=LIMIT, dimension_semantics=("arbitrary",)),
        cost_estimate=pl.CostEstimate(flops=2 * 10**10, bytes_accessed=4 * 10**7, transcendentals=0),
        name="rows_stage",
    )(need, src, *weights)


def final_kernel(
    pairs, live, need, src, w1h, w1l, w2h, w2l, gh, gl, done_rows, mine, theirs, tin, tout, lcol, lrow, sems
):
    KT = ((1,), (1,))
    step = pl.program_id(0)
    first, side = done_rows.shape[0], mine.shape[0]
    steps = (lrow.shape[0] - first) // PER
    copies = [
        pltpu.make_async_copy(done_rows, lrow.at[pl.ds(0, first)], sems.at[0]),
        pltpu.make_async_copy(mine, lcol.at[pl.ds(0, side)], sems.at[1]),
        pltpu.make_async_copy(theirs, lcol.at[pl.ds(side, side)], sems.at[2]),
    ]

    @pl.when(step == 0)
    def _():
        for copy in copies:
            copy.start()

    @pl.when(step < steps)
    def _():
        at = jnp.minimum(step, steps - 1)

        @pl.when(need[steps + at] > 0)
        def _():
            solve_tiles(src, w1h, w1l, w2h, w2l, gh, gl, put_into(lrow, first + at * PER))

    @pl.when(step == steps)
    def _():
        for copy in copies:
            copy.wait()

    @pl.when(step >= steps)
    def _():
        base = (step - steps) * GROUP
        for u in range(GROUP):
            slot = base + u

            @pl.when(slot < live[0])
            def _():
                a, b = pairs[slot], pairs[SLOTS + slot]
                tout[0, u] = tin[0, u] - dot(lrow[a], lcol[b], KT)

            @pl.when(slot >= live[0])
            def _():
                tout[0, u] = tin[0, u]


def final_stage(pairs, live, need, src, weights, done_rows, mine, theirs, trailing):
    count, slots = src.shape[0], trailing.shape[1]
    cs, ks = done_rows.shape[0] // PER, slots // GROUP
    tmap = lambda s, *_: (0, jnp.clip(s - cs, 0, ks - 1), 0, 0)
    return pl.pallas_call(
        final_kernel,
        out_shape=jax.ShapeDtypeStruct(trailing.shape, F32),
        grid_spec=pltpu.PrefetchScalarGridSpec(
            num_scalar_prefetch=3,
            grid=(cs + ks,),
            in_specs=[pl.BlockSpec((PER, 2, HALF, N), lambda s, *_: (cs + jnp.minimum(s, cs - 1), 0, 0, 0))]
            + [ONCE] * 6
            + [ANY] * 3
            + [pl.BlockSpec((1, GROUP, HALF, HALF), tmap)],
            out_specs=pl.BlockSpec((1, GROUP, HALF, HALF), tmap),
            scratch_shapes=[
                pltpu.VMEM((2 * mine.shape[0], HALF, 2 * N), BF16),
                pltpu.VMEM((count, HALF, 2 * N), BF16),
                pltpu.SemaphoreType.DMA((3,)),
            ],
        ),
        compiler_params=pltpu.CompilerParams(vmem_limit_bytes=LIMIT, dimension_semantics=("arbitrary",)),
        cost_estimate=pl.CostEstimate(flops=3 * 10**10, bytes_accessed=4 * 10**7, transcendentals=0),
        name="final_stage",
    )(pairs, live, need, src, *weights, done_rows, mine, theirs, trailing)


def spread(x, nrow, ncol):
    every = [(r, c) for r in range(nrow) for c in range(ncol)]
    half = ncol // 2
    flat = lambda r, c: r % nrow * ncol + c % ncol
    near, away = (
        lax.ppermute(x, ("row", "col"), [(flat(r, c + r + off), flat(r, c)) for r, c in every])
        for off in (0, half)
    )
    unit = jnp.stack([near, away], axis=0)
    up = lax.ppermute(unit, "row", [(r, (r + 2) % nrow) for r in range(nrow)])
    down = lax.ppermute(unit, "row", [(r, (r - 2) % nrow) for r in range(nrow)])
    row, col = lax.axis_index("row"), lax.axis_index("col")
    core = row % 2
    far = lax.ppermute(
        jnp.where(core == 0, up, down), "row", [(r, (r + (2 if r % 2 == 0 else -2)) % nrow) for r in range(nrow)]
    )
    mine = jnp.concatenate([unit, down, far, up], axis=0)
    theirs = lax.ppermute(mine, "row", [(r, r ^ 1) for r in range(nrow)])
    off = (jnp.arange(ncol, dtype=jnp.int32) - col) % ncol
    holder, side = off % half, off // half
    ahead = (holder // 2 - row // 2) % (nrow // 2)
    other = (holder % 2 != core).astype(jnp.int32)
    return mine, theirs, (other * mine.shape[0] + 2 * ahead + side).astype(jnp.int32)


def per_device(
    nrow, ncol, panel_first, panel_second, diag_first, bridge, diag_second, trailing, trail_pairs, live_count
):
    whole_first = lax.all_gather(diag_first, "col", axis=0, tiled=True)
    mine, theirs, where = spread(jnp.concatenate([bridge, diag_second], axis=0), nrow, ncol)
    both = jnp.stack([panel_first[0], panel_second[0]], axis=0)
    row_p = lax.all_gather(both, "col", axis=0)
    held, mine = lax.optimization_barrier((both, mine))
    up, down, far = (
        lax.ppermute(held, "row", [(r, (r + d) % nrow) for r in range(nrow)]) for d in (2, -2, nrow // 2)
    )
    row = lax.axis_index("row")
    pairs = trail_pairs[0]
    seat = 4 * (pairs[1] % 2 != row % 2).astype(jnp.int32) + (pairs[1] // 2 - row // 2) % (nrow // 2)
    active = jnp.arange(pairs.shape[1], dtype=jnp.int32) < live_count[0]
    group = jnp.arange(ncol // PER, dtype=jnp.int32)
    need = jnp.any((pairs[0][None] // PER == group[:, None]) & active[None], axis=1).astype(jnp.int32)
    seats = jnp.concatenate([pairs[0], seat]).astype(jnp.int32)
    whole_first, where, need, seats = lax.optimization_barrier((whole_first, where, need, seats))
    w1h, w1l = first_stage(whole_first)
    weights = (w1h, w1l, *second_stage(where, mine, theirs, w1h, w1l))
    lower_first, lower_second, ours = cols_stage((held, down, far, up), weights)
    others = lax.ppermute(ours, "row", [(r, r ^ 1) for r in range(nrow)])
    done_rows = rows_stage(need, row_p, weights)
    owned = final_stage(
        seats, live_count, need, row_p, weights, done_rows, ours, others, trailing
    )
    return lower_first, lower_second, owned


def solution(mesh):
    return jax.shard_map(
        functools.partial(per_device, mesh.shape["row"], mesh.shape["col"]),
        mesh=mesh,
        in_specs=(
            P(("row", "col"), None, None),
            P(("row", "col"), None, None),
            P("col", None),
            P("col", None),
            P("col", None),
            P(("row", "col"), None, None, None),
            P(("row", "col"), None, None),
            P(("row", "col")),
        ),
        out_specs=(
            P(("row", "col"), None, None),
            P(("row", "col"), None, None),
            P(("row", "col"), None, None, None),
        ),
        check_vma=False,
    )
```
